512 devices in a mesh: section: 16 (over z, x_hi), expert: 32 (over y, x_lo, core).
Axes of the slice: x: 4 (x_hi: 2, x_lo: 2; x = x_hi * 2 + x_lo), y: 8, z: 8, core: 2. Of those that a mesh axis runs over, the one named last changes fastest.
Arguments:
- fwd_sent: bfloat16 [16, 2048, 4096], P('section', 'expert'), may hold values from -6 to 6
- bwd_sent: bfloat16 [16, 2048, 4096], P('section', 'expert'), may hold values from -6 to 6
- bwd_saved: bfloat16 [16, 2048, 4096], P('section', 'expert'), may hold values from -6 to 6
- fwd_routes: int32 [16, 2048, 8], P('section', 'expert'), may hold values from 0 to 127, all different within a row; in each aligned block of 64 rows (0 to 63, 64 to 127, ..., all dimensions but the last counted through in order) at most 8 rows name the same one
- bwd_routes: int32 [16, 2048, 8], P('section', 'expert'), may hold values from 0 to 127, all different within a row; in each aligned block of 64 rows (0 to 63, 64 to 127, ..., all dimensions but the last counted through in order) at most 8 rows name the same one
- fwd_logits: float32 [16, 2048, 128], P('section', 'expert'), may hold values from -3 to 330
- bwd_logits: float32 [16, 2048, 128], P('section', 'expert'), may hold values from -3 to 330
- norm_gain: bfloat16 [16, 4096], P('section'), may hold values from 0.5 to 1.5
- w_gate: bfloat16 [16, 4096, 3072], P('section', None, 'expert'), may hold values from -0.09375 to 0.09375
- w_up: bfloat16 [16, 4096, 3072], P('section', None, 'expert'), may hold values from -0.09375 to 0.09375
- w_down: bfloat16 [16, 3072, 4096], P('section', 'expert'), may hold values from -0.4375 to 0.4375
Outputs:
- fwd_out: bfloat16 [16, 2048, 4096], P('section', 'expert')
- bwd_out: bfloat16 [16, 2048, 4096], P('section', 'expert')
- balance: float32 [16, 128], P('section')
The draws below stay inside these ranges and needn't reach their ends.
Inputs may be any that keep to these rules, and one draw needn't show every extreme that they name: `fwd_routes`: each token names 8 different experts; among the 64 tokens of one index of expert no expert is named more than 8 times, a bound that some block reaches. `bwd_routes`: as for fwd_routes.
All inputs are finite; a program needn't handle non-finite values.
Results may differ from the reference program's by a relative error of at most 0.0045.
Values may be sent and summed in bfloat16 or wider, within the bound.
No kernel may reach another device: no remote copies, remote signals or barrier semaphores. Data moves between devices by JAX's collectives and lax.ppermute only.
A program may use at most 64 MiB of HBM per device.

```python
import math
import jax
import jax.numpy as jnp
import numpy as np
from jax import lax

D = 4096
FF_WIN = 1536
EXPERTS = 128
TOPK = 8
EXP_WIN = 2
TOK_DEV = 64
CAP = 8
SECTIONS = 16
TOKENS = 2048
H_DEV = 96
N_EXPERT = 32


def draw_logits(key):
    base_key, lead_key = jax.random.split(key, 2)
    shape = (SECTIONS, TOKENS, EXPERTS)
    expert_ids = jnp.arange(EXPERTS, dtype=jnp.int32)
    computed = (expert_ids < EXP_WIN)[None, None, :]
    leading = jax.random.uniform(lead_key, shape, jnp.float32, 1.5, 3.5)
    base = jnp.clip(0.7 * jax.random.normal(base_key, shape, jnp.float32), -2.5, 2.5)
    return jnp.where(computed, leading, base)


def draw_fwd_logits(key, part):
    return draw_logits(jax.random.fold_in(key, 11))


def draw_bwd_logits(key, part):
    return draw_logits(jax.random.fold_in(key, 23))


def steps_of(key, extent, shards, least, largest):
    def one(dim, shards_of):
        heights = jax.random.uniform(jax.random.fold_in(jax.random.fold_in(key, 6), dim), (shards_of,), jnp.float32, least / len(shards), largest / len(shards))
        return jnp.repeat(jnp.exp(heights), extent[dim] // shards_of).reshape((-1,) + (1,) * (len(extent) - dim - 1))

    factor_of = one(*shards[0])
    for cut in shards[1:]:
        factor_of = factor_of * one(*cut)
    return factor_of


def routed_block(rng, own, number, rows, number_of, top, bound, lean):
    ranking = jax.random.permutation(rng, number_of)
    crowded, common = shares(number_of, rows * top, bound, lean, True), shares(number_of, rows * top, bound, lean, False)
    places = jnp.arange(number_of)

    def named(tallies, turn):
        used = int((tallies > 0).sum())
        fixed = max(1, used // 4)
        moved = fixed + (places - fixed + turn * (used - fixed)) % max(1, number_of - fixed)
        return jnp.zeros((number_of,), jnp.int32).at[ranking[jnp.where(places < fixed, places, moved)]].set(jnp.asarray(tallies, jnp.int32))

    tallies = jnp.where(number % 4 == 0, named(crowded, number // 4), named(common, number - number // 4 - 1))
    mixed = jax.random.permutation(jax.random.fold_in(own, 3), number_of)
    giver, taker = mixed[0:number_of // 2 * 2:2], mixed[1:number_of // 2 * 2:2]
    slack = jnp.minimum(tallies[giver] - 1, bound - tallies[taker]) // 2
    slack = jnp.where((giver == ranking[0]) | (taker == ranking[0]) | (tallies[taker] == 0), 0, jnp.maximum(slack, 0))
    moved = jax.random.randint(jax.random.fold_in(own, 4), (number_of // 2,), 0, 1 << 20) % (slack + 1)
    tallies = tallies.at[giver].add(-moved).at[taker].add(moved)
    items = jnp.searchsorted(jnp.cumsum(tallies), jnp.arange(rows * top), side="right").astype(jnp.int32)
    grid = items.reshape(top, rows).T
    grid = grid[jax.random.permutation(jax.random.fold_in(own, 1), rows)]
    turn = jax.random.randint(jax.random.fold_in(own, 2), (rows, 1), 0, top)
    return jnp.take_along_axis(grid, (jnp.arange(top)[None, :] + turn) % top, axis=1)


def shares(number_of, total, most, skew, full):
    weights = [(1 << 20) // math.isqrt(standing ** skew) + 1 for standing in range(1, number_of + 1)]
    largest = most if full else min(most, max(-(-total // number_of), total * weights[0] // sum(weights)))
    least = 1 if total - largest >= number_of - 1 else 0
    holding, surplus = [largest] + [least] * (number_of - 1), total - largest - least * (number_of - 1)
    while surplus > 0:
        movable = [i for i in range(1, number_of) if holding[i] < largest] or [i for i in range(1, number_of) if holding[i] < most]
        pool, left = sum([weights[i] for i in movable]), surplus
        for i in movable:
            more = min(most - holding[i], max(1, left * weights[i] // pool), surplus)
            holding[i] = holding[i] + more
            surplus = surplus - more
    return np.array(holding)


def centred(own_key, shape, deviation, most, pieces=(), held_as=jnp.bfloat16):
    gain = steps_of(own_key, shape, pieces, -0.22, 0.18) if pieces else 1.0
    result = jax.random.normal(own_key, shape, jnp.float32) * deviation * gain
    return jnp.minimum(jnp.maximum(result, -most), most).astype(held_as)


def setup_inputs(seed: int = 0) -> dict:
    key_list = jax.random.split(jax.random.key(seed), 12)
    fwd_sent = centred(key_list[0], (SECTIONS, TOKENS, D), 1.0, 6.0, ((0, 16), (1, 32)))
    bwd_sent = centred(key_list[1], (SECTIONS, TOKENS, D), 1.0, 6.0, ((0, 16), (1, 32)))
    bwd_saved = centred(key_list[2], (SECTIONS, TOKENS, D), 1.0, 6.0, ((0, 16), (1, 32)))
    fwd_routes_keys = jax.random.split(jax.random.fold_in(key_list[3], 1), SECTIONS * TOKENS // TOK_DEV)
    fwd_routes_turns = jax.random.permutation(jax.random.fold_in(key_list[3], 3), SECTIONS * TOKENS // TOK_DEV)
    fwd_routes = jax.vmap(lambda own, number: routed_block(jax.random.fold_in(key_list[3], 2), own, number, TOK_DEV, EXPERTS, TOPK, CAP, 1))(fwd_routes_keys, fwd_routes_turns).reshape((SECTIONS, TOKENS, TOPK))
    bwd_routes_keys = jax.random.split(jax.random.fold_in(key_list[4], 1), SECTIONS * TOKENS // TOK_DEV)
    bwd_routes_turns = jax.random.permutation(jax.random.fold_in(key_list[4], 3), SECTIONS * TOKENS // TOK_DEV)
    bwd_routes = jax.vmap(lambda own, number: routed_block(jax.random.fold_in(key_list[4], 2), own, number, TOK_DEV, EXPERTS, TOPK, CAP, 1))(bwd_routes_keys, bwd_routes_turns).reshape((SECTIONS, TOKENS, TOPK))
    fwd_logits = draw_fwd_logits(jax.random.fold_in(key_list[11], 71), 0)
    bwd_logits = draw_bwd_logits(jax.random.fold_in(key_list[11], 71), 0)
    norm_gain = jnp.clip(0.5 + 1.0 * jax.random.uniform(key_list[7], (SECTIONS, D), jnp.float32) ** steps_of(key_list[7], (SECTIONS, D), ((0, 16),), -0.2, 0.2), 0.5, 1.5).astype(jnp.bfloat16)
    w_gate = centred(key_list[8], (SECTIONS, D, EXP_WIN * FF_WIN), D ** -0.5, 0.09375, ((0, 16), (2, 32)))
    w_up = centred(key_list[9], (SECTIONS, D, EXP_WIN * FF_WIN), D ** -0.5, 0.09375, ((0, 16), (2, 32)))
    w_down = centred(key_list[10], (SECTIONS, EXP_WIN * FF_WIN, D), (FF_WIN // 8) ** -0.5, 0.4375, ((0, 16), (1, 32)))
    return dict(fwd_sent=fwd_sent, bwd_sent=bwd_sent, bwd_saved=bwd_saved, fwd_routes=fwd_routes, bwd_routes=bwd_routes, fwd_logits=fwd_logits, bwd_logits=bwd_logits, norm_gain=norm_gain, w_gate=w_gate, w_up=w_up, w_down=w_down)


epsilon = 1e-06

def norm_rows(values, gain_row):
    widened = values.astype(jnp.float32)
    inverse = lax.rsqrt(lax.optimization_barrier(jnp.mean(widened * widened, axis=-1, keepdims=True)) + epsilon)
    normed = (widened * inverse * gain_row.astype(jnp.float32)).astype(jnp.bfloat16)
    return (normed, widened, inverse)

def slot_tables(routes, logits):
    tokens_here = routes.shape[0]
    chosen = jnp.take_along_axis(logits, routes, axis=1)
    gates = jax.nn.softmax(chosen, axis=1)
    match = (routes[:, :, None] == jnp.arange(EXP_WIN, dtype=jnp.int32)[None, None, :]).astype(jnp.int32)
    flat = match.reshape(tokens_here * TOPK, EXP_WIN)
    earlier = (jnp.cumsum(flat, axis=0) - flat).reshape(tokens_here, TOPK, EXP_WIN)
    placed = match[..., None] * (earlier[..., None] == jnp.arange(CAP, dtype=jnp.int32)).astype(jnp.int32)
    select = lax.optimization_barrier(jnp.sum(placed, axis=1)).astype(jnp.float32)
    gate_slot = lax.optimization_barrier(jnp.sum(placed.astype(jnp.float32) * gates[:, :, None, None], axis=(0, 1)))
    return (select, gate_slot)

def expert_forward(rows, gate_w, up_w, down_w):
    groups = FF_WIN // H_DEV
    gate_pre = jnp.dot(rows, gate_w, preferred_element_type=jnp.float32)
    up_pre = jnp.dot(rows, up_w, preferred_element_type=jnp.float32)
    hidden = (jax.nn.silu(gate_pre) * up_pre).astype(jnp.bfloat16)
    parts = jnp.einsum('rsh,shd->rsd', hidden.reshape(-1, groups, H_DEV).astype(jnp.float32), down_w.reshape(groups, H_DEV, D).astype(jnp.float32))
    parts = lax.optimization_barrier(parts.astype(jnp.bfloat16)).astype(jnp.float32)
    return lax.optimization_barrier(jnp.sum(parts, axis=1))

def expert_backward(rows, grads, gate_w, up_w, down_w):
    groups = FF_WIN // H_DEV
    gate_pre = jnp.dot(rows, gate_w, preferred_element_type=jnp.float32)
    up_pre = jnp.dot(rows, up_w, preferred_element_type=jnp.float32)
    sigma = jax.nn.sigmoid(gate_pre)
    d_hidden = jnp.dot(grads, down_w.T, preferred_element_type=jnp.float32)
    d_gate = (d_hidden * up_pre * sigma * (1.0 + gate_pre * (1.0 - sigma))).astype(jnp.bfloat16)
    d_up = (d_hidden * gate_pre * sigma).astype(jnp.bfloat16)
    parts = jnp.einsum('rsh,dsh->rsd', d_gate.reshape(-1, groups, H_DEV).astype(jnp.float32), gate_w.reshape(D, groups, H_DEV).astype(jnp.float32))
    parts = parts + jnp.einsum('rsh,dsh->rsd', d_up.reshape(-1, groups, H_DEV).astype(jnp.float32), up_w.reshape(D, groups, H_DEV).astype(jnp.float32))
    parts = lax.optimization_barrier(parts.astype(jnp.bfloat16)).astype(jnp.float32)
    return lax.optimization_barrier(jnp.sum(parts, axis=1))

def one_section(packed):
    x_in, upstream, saved, froutes, broutes, flogits, blogits, gain_row, gate_w, up_w, down_w = packed
    blocks = N_EXPERT
    normed = norm_rows(x_in, gain_row)[0]
    fsel, fgate = jax.vmap(slot_tables)(froutes.reshape(blocks, TOK_DEV, TOPK), flogits.reshape(blocks, TOK_DEV, EXPERTS))
    frows = jnp.einsum('btec,btd->becd', fsel, normed.reshape(blocks, TOK_DEV, D).astype(jnp.float32)).astype(jnp.bfloat16)
    fexp = jnp.stack([expert_forward(frows[:, e].reshape(blocks * CAP, D), gate_w[:, e * FF_WIN:(e + 1) * FF_WIN], up_w[:, e * FF_WIN:(e + 1) * FF_WIN], down_w[e * FF_WIN:(e + 1) * FF_WIN, :]).reshape(blocks, CAP, D) for e in range(EXP_WIN)], axis=1)
    mixed = jnp.einsum('btec,becd->btd', fsel * fgate[:, None], fexp).reshape(TOKENS, D)
    fwd_out = (x_in.astype(jnp.float32) + mixed).astype(jnp.bfloat16)
    saved_normed, saved_wide, saved_inv = norm_rows(saved, gain_row)
    bsel, bgate = jax.vmap(slot_tables)(broutes.reshape(blocks, TOK_DEV, TOPK), blogits.reshape(blocks, TOK_DEV, EXPERTS))
    brows = jnp.einsum('btec,btd->becd', bsel, saved_normed.reshape(blocks, TOK_DEV, D).astype(jnp.float32)).astype(jnp.bfloat16)
    grows = jnp.einsum('btec,btd->becd', bsel, upstream.reshape(blocks, TOK_DEV, D).astype(jnp.float32))
    grows = (grows * bgate[..., None]).astype(jnp.bfloat16)
    bexp = jnp.stack([expert_backward(brows[:, e].reshape(blocks * CAP, D), grows[:, e].reshape(blocks * CAP, D), gate_w[:, e * FF_WIN:(e + 1) * FF_WIN], up_w[:, e * FF_WIN:(e + 1) * FF_WIN], down_w[e * FF_WIN:(e + 1) * FF_WIN, :]).reshape(blocks, CAP, D) for e in range(EXP_WIN)], axis=1)
    d_normed = jnp.einsum('btec,becd->btd', bsel, bexp).reshape(TOKENS, D)
    weighted = gain_row.astype(jnp.float32) * d_normed
    d_saved = saved_inv * weighted - saved_wide * saved_inv ** 3 * lax.optimization_barrier(jnp.mean(saved_wide * weighted, axis=-1, keepdims=True))
    bwd_out = (upstream.astype(jnp.float32) + d_saved).astype(jnp.bfloat16)
    counts = lax.optimization_barrier(jnp.sum((froutes[:, :, None] == jnp.arange(EXPERTS, dtype=jnp.int32)[None, None, :]).astype(jnp.float32), axis=(0, 1)))
    prob_sums = lax.optimization_barrier(jnp.sum(jax.nn.softmax(flogits, axis=1), axis=0))
    balance = EXPERTS * (counts / (TOKENS * TOPK)) * (prob_sums / TOKENS)
    return (fwd_out, bwd_out, balance)

def reference(fwd_sent, bwd_sent, bwd_saved, fwd_routes, bwd_routes, fwd_logits, bwd_logits, norm_gain, w_gate, w_up, w_down):
    x_all = jnp.roll(fwd_sent, 1, axis=0)
    upstream_all = jnp.roll(bwd_sent, -1, axis=0)
    fwd_out, bwd_out, balance = lax.map(one_section, (x_all, upstream_all, bwd_saved, fwd_routes, bwd_routes, fwd_logits, bwd_logits, norm_gain, w_gate, w_up, w_down))
    return (fwd_out, bwd_out, balance)
```

```python
import jax
import jax.numpy as jnp
from jax import lax
from jax.experimental import pallas as pl
from jax.experimental.pallas import tpu as pltpu
from jax.sharding import Mesh, PartitionSpec as P

EXPERTS = 128
TOPK = 8
EXP_WIN = 2
CAP = 8
SLOTS = EXP_WIN * CAP
EPS = 1e-06
exact = lax.Precision.HIGHEST
f32 = jnp.float32
bf16 = jnp.bfloat16
NT = (((1,), (1,)), ((), ()))
PARAMS = pltpu.CompilerParams(vmem_limit_bytes=48 << 20)
EXPERT_AXES = ("y", "xl", "core")


def kernel_call(body, outs, *args):
    return pl.pallas_call(body, out_shape=outs, compiler_params=PARAMS)(*args)


def shape(dims, dtype):
    return jax.ShapeDtypeStruct(dims, dtype)


def iota(dims, axis):
    return lax.broadcasted_iota(jnp.int32, dims, axis)


def slot_tables(routes_t, logits):
    tokens, experts = logits.shape
    ids = iota((experts, tokens), 0)
    hot_t = jnp.zeros((experts, tokens), f32)
    for k in range(TOPK):
        hot_t = hot_t + jnp.where(ids == routes_t[k : k + 1, :], 1.0, 0.0)
    rows, cols = iota((tokens, tokens), 0), iota((tokens, tokens), 1)
    eye = jnp.where(rows == cols, 1.0, 0.0).astype(bf16)
    hot = lax.dot_general(eye, hot_t.astype(bf16), NT, preferred_element_type=f32)
    chosen = jnp.where(hot > 0.5, logits, -jnp.inf)
    powers = jnp.exp(chosen - jnp.max(chosen, axis=1, keepdims=True))
    gates = powers / jnp.sum(powers, axis=1, keepdims=True)
    before = jnp.where(rows < cols, 1.0, 0.0).astype(bf16)
    first = hot_t[0:8, :]
    earlier = jnp.dot(first.astype(bf16), before, preferred_element_type=f32)
    slot = iota((CAP, tokens), 0).astype(f32)
    select = jnp.concatenate(
        [
            jnp.where((earlier[e : e + 1, :] == slot) & (first[e : e + 1, :] > 0.5), 1.0, 0.0)
            for e in range(EXP_WIN)
        ],
        axis=0,
    )
    select_t = lax.dot_general(eye, select.astype(bf16), NT, preferred_element_type=f32)
    picked = jnp.dot(select, gates, precision=exact, preferred_element_type=f32)
    own = iota((SLOTS, experts), 1) == iota((SLOTS, experts), 0) // CAP
    gate_slot = jnp.sum(jnp.where(own, picked, 0.0), axis=1, keepdims=True)
    return hot, select.astype(bf16), select_t.astype(bf16), gate_slot


def spread(send_ref, rows):
    stops = send_ref.shape[0]
    for i in range(stops):
        e = i * EXP_WIN // stops
        send_ref[i, :, :] = rows[e * CAP : (e + 1) * CAP, :]


def normed_rows(rows, gain):
    inverse = lax.rsqrt(jnp.mean(rows * rows, axis=1, keepdims=True) + EPS)
    return (rows * inverse * gain).astype(bf16), inverse


def prepare_body(
    saved, gain, broutes, blogits, froutes, flogits,
    send, picked, inverse_out, bsel, bsel_t, bgate, fsel, fsel_t, fgate, usage,
):
    wide = (SLOTS, EXPERTS)
    _, select, select_t, gate = slot_tables(broutes[...], blogits[...])
    bsel[...], bsel_t[...], bgate[...] = select, select_t, jnp.broadcast_to(gate, wide)
    rows = jnp.dot(select, saved[...], preferred_element_type=f32)
    normed, inverse = normed_rows(rows, gain[...].astype(f32))
    picked[...] = rows.astype(bf16)
    inverse_out[...] = jnp.broadcast_to(inverse, wide)
    spread(send, normed)
    logits = flogits[...]
    hot, select, select_t, gate = slot_tables(froutes[...], logits)
    fsel[...], fsel_t[...], fgate[...] = select, select_t, jnp.broadcast_to(gate, wide)
    powers = jnp.exp(logits - jnp.max(logits, axis=1, keepdims=True))
    probs = powers / jnp.sum(powers, axis=1, keepdims=True)
    usage[...] = jnp.concatenate(
        [jnp.sum(hot, axis=0, keepdims=True), jnp.sum(probs, axis=0, keepdims=True)], axis=0
    )


def grad_rows_body(upstream, select, gate, send):
    rows = jnp.dot(select[...], upstream[...], preferred_element_type=f32)
    spread(send, (rows * gate[:, 0:1]).astype(bf16))


def fwd_rows_body(x_in, select, gain, send):
    rows = jnp.dot(select[...], x_in[...], preferred_element_type=f32)
    spread(send, normed_rows(rows, gain[...].astype(f32))[0])


def nt(a, b):
    return lax.dot_general(a, b, NT, preferred_element_type=f32)


COLS = 512


def fwd_expert_body(mine, other, slab, slab2, out_mine, out_other):
    hid = slab.shape[0] // 3
    for rows, out in ((mine[...], out_mine), (other[...], out_other)):
        hidden = []
        for w in (slab, slab2):
            pre = nt(rows, w[0 : 2 * hid, :])
            hidden.append((jax.nn.silu(pre[:, :hid]) * pre[:, hid:]).astype(bf16))
        for c in range(0, out.shape[1], COLS):
            part = sum(
                jnp.dot(h, w[2 * hid :, c : c + COLS], preferred_element_type=f32)
                for h, w in zip(hidden, (slab, slab2))
            )
            out[:, c : c + COLS] = part.astype(bf16)


def bwd_expert_body(mine, other, gmine, gother, slab, slab2, out_mine, out_other):
    hid = slab.shape[0] // 3
    for rows, grads, out in (
        (mine[...], gmine[...], out_mine),
        (other[...], gother[...], out_other),
    ):
        back = []
        for w in (slab, slab2):
            pre = nt(rows, w[0 : 2 * hid, :])
            d_hidden = nt(grads, w[2 * hid :, :])
            a, b = pre[:, :hid], pre[:, hid:]
            sigma = jax.nn.sigmoid(a)
            d_gate = (d_hidden * b * sigma * (1.0 + a * (1.0 - sigma))).astype(bf16)
            d_up = (d_hidden * a * sigma).astype(bf16)
            back.append((d_gate, d_up))
        for c in range(0, out.shape[1], COLS):
            part = jnp.zeros((out.shape[0], COLS), f32)
            for (d_gate, d_up), w in zip(back, (slab, slab2)):
                part = part + jnp.dot(d_gate, w[0:hid, c : c + COLS], preferred_element_type=f32)
                part = part + jnp.dot(
                    d_up, w[hid : 2 * hid, c : c + COLS], preferred_element_type=f32
                )
            out[:, c : c + COLS] = part.astype(bf16)


def gathered(parts):
    stops = parts.shape[0]
    half = stops // EXP_WIN
    return jnp.concatenate(
        [
            sum(parts[e * half + i, :, :].astype(f32) for i in range(half))
            for e in range(EXP_WIN)
        ],
        axis=0,
    )


def placed(select_t, rows):
    high = rows.astype(bf16)
    rest = rows - high.astype(f32)
    mid = rest.astype(bf16)
    low = (rest - mid.astype(f32)).astype(bf16)
    return sum(jnp.dot(select_t, p, preferred_element_type=f32) for p in (low, mid, high))


def fwd_out_body(parts, select_t, gate, x_in, out):
    rows = gathered(parts) * gate[:, 0:1]
    out[...] = (x_in[...].astype(f32) + placed(select_t[...], rows)).astype(bf16)


def bwd_out_body(parts, select_t, picked, inverse, gain, upstream, out):
    weighted = gain[...].astype(f32) * gathered(parts)
    inv = inverse[:, 0:1]
    x = picked[...].astype(f32)
    rows = inv * weighted - x * (inv * inv * inv) * jnp.mean(x * weighted, axis=1, keepdims=True)
    out[...] = (upstream[...].astype(f32) + placed(select_t[...], rows)).astype(bf16)


def shifted(block, axis, distance):
    n = lax.axis_size(axis)
    return lax.ppermute(block, axis, [((i - distance) % n, i) for i in range(n)])


def over_y(block):
    return lax.all_to_all(block, "y", split_axis=0, concat_axis=0, tiled=True)


def body(
    fwd_sent, bwd_sent, bwd_saved, fwd_routes, bwd_routes, fwd_logits, bwd_logits,
    norm_gain, w_gate, w_up, w_down,
):
    stops = lax.axis_size("y")
    tokens, width = fwd_sent.shape[1:]
    upstream = shifted(bwd_sent[0], "section", -1)
    x_in = shifted(fwd_sent[0], "section", 1)
    slab = jnp.concatenate([w_gate[0].T, w_up[0].T, w_down[0]], axis=0)
    slab2 = shifted(slab, "core", 1)
    saved = bwd_saved[0]
    sent = shape((stops, CAP, width), bf16)
    sel, sel_t = shape((SLOTS, tokens), bf16), shape((tokens, SLOTS), bf16)
    wide = shape((SLOTS, EXPERTS), f32)
    saved_send, picked, inverse, bsel, bsel_t, bgate, fsel, fsel_t, fgate, usage = kernel_call(
        prepare_body,
        (sent, shape((SLOTS, width), bf16), wide, sel, sel_t, wide, sel, sel_t, wide,
         shape((2, EXPERTS), f32)),
        saved, norm_gain, bwd_routes[0].T, bwd_logits[0], fwd_routes[0].T, fwd_logits[0],
    )
    saved_mine = over_y(saved_send).reshape(-1, width)
    saved_other = shifted(saved_mine, "xl", 1)
    grad_send = kernel_call(grad_rows_body, sent, upstream, bsel, bgate)
    grad_mine = over_y(grad_send).reshape(-1, width)
    grad_other = shifted(grad_mine, "xl", 1)
    fwd_send = kernel_call(fwd_rows_body, sent, x_in, fsel, norm_gain)
    fwd_mine = over_y(fwd_send).reshape(-1, width)
    fwd_other = shifted(fwd_mine, "xl", 1)
    result = shape(saved_mine.shape, bf16)
    back_mine, back_other = kernel_call(
        bwd_expert_body, (result, result), saved_mine, saved_other, grad_mine, grad_other, slab, slab2
    )
    back = (back_mine.astype(f32) + shifted(back_other, "xl", 1).astype(f32)).astype(bf16)
    back_parts = over_y(back.reshape(stops, CAP, width))
    out_mine, out_other = kernel_call(
        fwd_expert_body, (result, result), fwd_mine, fwd_other, slab, slab2
    )
    outs = (out_mine.astype(f32) + shifted(out_other, "xl", 1).astype(f32)).astype(bf16)
    out_parts = over_y(outs.reshape(stops, CAP, width))
    full = shape((tokens, width), bf16)
    bwd_out = kernel_call(
        bwd_out_body, full, back_parts, bsel_t, picked, inverse, norm_gain, upstream
    )
    fwd_out = kernel_call(fwd_out_body, full, out_parts, fsel_t, fgate, x_in)
    devices = lax.axis_size(EXPERT_AXES)
    shared = lax.all_to_all(
        jnp.broadcast_to(usage[None], (devices, 2, EXPERTS)),
        EXPERT_AXES, split_axis=0, concat_axis=0, tiled=True,
    )
    counts, prob_sums = jnp.sum(shared, axis=0)
    tokens_all = tokens * devices
    balance = EXPERTS * (counts / (tokens_all * TOPK)) * (prob_sums / tokens_all)
    return (fwd_out[None], bwd_out[None], balance[None])


def solution(mesh):
    sections = mesh.shape["section"]
    grid = mesh.devices.reshape(sections, -1, 2, 2)
    inner = Mesh(grid, ("section",) + EXPERT_AXES)
    rows = P("section", EXPERT_AXES, None)
    return jax.shard_map(
        body,
        mesh=inner,
        in_specs=(
            rows, rows, rows, rows, rows, rows, rows,
            P("section", None),
            P("section", None, EXPERT_AXES),
            P("section", None, EXPERT_AXES),
            rows,
        ),
        out_specs=(rows, rows, P("section", None)),
        check_vma=False,
    )
```

```python
import jax
import jax.numpy as jnp
from jax import lax
from jax.experimental import pallas as pl
from jax.experimental.pallas import tpu as pltpu
from jax.sharding import Mesh, PartitionSpec as P

EXPERTS = 128
TOPK = 8
EXP_WIN = 2
CAP = 8
SLOTS = EXP_WIN * CAP
EPS = 1e-06
exact = lax.Precision.HIGHEST
f32 = jnp.float32
bf16 = jnp.bfloat16
NT = (((1,), (1,)), ((), ()))
PARAMS = pltpu.CompilerParams(vmem_limit_bytes=48 << 20)
EXPERT_AXES = ("y", "xl", "core")


def shape(dims, dtype):
    return jax.ShapeDtypeStruct(dims, dtype)


def iota(dims, axis):
    return lax.broadcasted_iota(jnp.int32, dims, axis)


def slot_tables(routes_t, logits):
    tokens, experts = logits.shape
    ids = iota((experts, tokens), 0)
    hot_t = jnp.zeros((experts, tokens), f32)
    for k in range(TOPK):
        hot_t = hot_t + jnp.where(ids == routes_t[k : k + 1, :], 1.0, 0.0)
    rows, cols = iota((tokens, tokens), 0), iota((tokens, tokens), 1)
    eye = jnp.where(rows == cols, 1.0, 0.0).astype(bf16)
    hot = lax.dot_general(eye, hot_t.astype(bf16), NT, preferred_element_type=f32)
    chosen = jnp.where(hot > 0.5, logits, -jnp.inf)
    powers = jnp.exp(chosen - jnp.max(chosen, axis=1, keepdims=True))
    gates = powers / jnp.sum(powers, axis=1, keepdims=True)
    before = jnp.where(rows < cols, 1.0, 0.0).astype(bf16)
    first = hot_t[0:8, :]
    earlier = jnp.dot(first.astype(bf16), before, preferred_element_type=f32)
    slot = iota((CAP, tokens), 0).astype(f32)
    select = jnp.concatenate(
        [
            jnp.where((earlier[e : e + 1, :] == slot) & (first[e : e + 1, :] > 0.5), 1.0, 0.0)
            for e in range(EXP_WIN)
        ],
        axis=0,
    )
    select_t = lax.dot_general(eye, select.astype(bf16), NT, preferred_element_type=f32)
    picked = jnp.dot(select, gates, precision=exact, preferred_element_type=f32)
    own = iota((SLOTS, experts), 1) == iota((SLOTS, experts), 0) // CAP
    gate_slot = jnp.sum(jnp.where(own, picked, 0.0), axis=1, keepdims=True)
    return hot, select.astype(bf16), select_t.astype(bf16), gate_slot


HBM = pl.BlockSpec(memory_space=pltpu.HBM)
VMEM = pl.BlockSpec(memory_space=pltpu.VMEM)


def in_hbm(dims, dtype):
    return pltpu.HBM(dims, dtype)


def kernel_call(body, outs, in_specs, out_specs, scratch, *args):
    args = [
        pltpu.with_memory_space_constraint(v, pltpu.HBM) if spec is HBM else v
        for v, spec in zip(args, in_specs)
    ]
    return pl.pallas_call(
        body, out_shape=outs, in_specs=in_specs, out_specs=out_specs, scratch_shapes=scratch,
        compiler_params=PARAMS,
    )(*args)


def started(sems, *pairs):
    copies = [pltpu.make_async_copy(src, dst, sems.at[i]) for i, (src, dst) in enumerate(pairs)]
    for copy in copies:
        copy.start()
    return copies


def wait_all(copies):
    for copy in copies:
        copy.wait()


def normed_rows(rows, gain):
    inverse = lax.rsqrt(jnp.mean(rows * rows, axis=1, keepdims=True) + EPS)
    return (rows * inverse * gain).astype(bf16), inverse


def by_expert(stops):
    return [(i, i * EXP_WIN // stops * CAP) for i in range(stops)]


def prepare_body(
    saved_h, gain_h, broutes_h, blogits_h, froutes_h, flogits_h,
    send, picked, columns, rows16, usage,
    saved, gain, broutes, blogits, froutes, flogits, sems,
):
    copies = started(
        sems, (broutes_h, broutes), (blogits_h, blogits), (froutes_h, froutes),
        (flogits_h, flogits), (gain_h, gain), (saved_h, saved),
    )
    wait_all(copies[:4])
    _, select, bselect_t, bgate = slot_tables(broutes[...], blogits[...])
    logits = flogits[...]
    hot, _, fselect_t, fgate = slot_tables(froutes[...], logits)
    powers = jnp.exp(logits - jnp.max(logits, axis=1, keepdims=True))
    probs = powers / jnp.sum(powers, axis=1, keepdims=True)
    usage[...] = jnp.concatenate(
        [jnp.sum(hot, axis=0, keepdims=True), jnp.sum(probs, axis=0, keepdims=True)], axis=0
    )
    wait_all(copies[4:])
    rows = jnp.dot(select, saved[...], preferred_element_type=f32)
    normed, inverse = normed_rows(rows, gain[...].astype(f32))
    picked[...] = rows.astype(bf16)
    columns[0, :, :] = bselect_t
    columns[1, :, :] = fselect_t
    wide = (SLOTS, EXPERTS)
    rows16[0, :, :] = jnp.broadcast_to(bgate, wide)
    rows16[1, :, :] = jnp.broadcast_to(fgate, wide)
    rows16[2, :, :] = jnp.broadcast_to(inverse, wide)
    for i, r in by_expert(send.shape[0]):
        send[i, :, :] = normed[r : r + CAP, :]


def rows_body(x_in, upstream, columns_h, rows16_h, gain_h, send, columns, gates, gain, sems):
    copies = started(sems, (columns_h, columns), (rows16_h.at[0], gates), (gain_h, gain))
    copies[0].wait()

    def chosen(i, block):
        return lax.dot_general(
            columns[i, :, :], block[...], (((0,), (0,)), ((), ())), preferred_element_type=f32
        )

    rows = chosen(1, x_in)
    grads = chosen(0, upstream)
    wait_all(copies[1:])
    normed = normed_rows(rows, gain[...].astype(f32))[0]
    grads = (grads * gates[:, 0:1]).astype(bf16)
    for i, r in by_expert(send.shape[0]):
        send[i, 0:CAP, :] = normed[r : r + CAP, :]
        send[i, CAP : 2 * CAP, :] = grads[r : r + CAP, :]


COLS = 512


def nt(a, b):
    return lax.dot_general(a, b, NT, preferred_element_type=f32)


def hidden_terms(saved, mixed, slab):
    hid = slab.shape[0] // 3
    kept = nt(saved, slab[0 : 2 * hid, :])
    pre = nt(mixed, slab[...]).reshape(-1, 2 * CAP, 3 * hid)
    forward, grads = pre[:, 0:CAP, :], pre[:, CAP:, :]
    h = jax.nn.silu(forward[:, :, :hid]) * forward[:, :, hid : 2 * hid]
    kept = kept.reshape(-1, CAP, 2 * hid)
    a, b, d_hidden = kept[:, :, :hid], kept[:, :, hid:], grads[:, :, 2 * hid :]
    sigma = jax.nn.sigmoid(a)
    d_gate = d_hidden * b * sigma * (1.0 + a * (1.0 - sigma))
    d_up = d_hidden * a * sigma
    none = jnp.zeros_like(h)
    top = jnp.concatenate([none, none, h], axis=2)
    low = jnp.concatenate([d_gate, d_up, none], axis=2)
    return jnp.concatenate([top, low], axis=1).reshape(-1, 3 * hid).astype(bf16)


def expert_first_body(saved_h, mixed_h, slab_h, slab2_h, out, saved, mixed, slab, slab2, sems):
    copies = started(
        sems, (saved_h, saved), (mixed_h, mixed), (slab_h, slab), (slab2_h, slab2)
    )
    wait_all(copies[:3])
    left = hidden_terms(saved[...], mixed[...], slab)
    copies[3].wait()
    left2 = hidden_terms(saved[...], mixed[...], slab2)
    for c in range(0, out.shape[1], COLS):
        cut = slice(c, c + COLS)
        part = jnp.dot(left, slab[:, cut], preferred_element_type=f32)
        out[:, cut] = part + jnp.dot(left2, slab2[:, cut], preferred_element_type=f32)


def expert_second_body(
    saved_h, mixed_h, slab_h, slab2_h, part_h, out, saved, mixed, slab, slab2, first, sems
):
    copies = started(
        sems, (saved_h, saved), (mixed_h, mixed), (slab_h, slab), (slab2_h, slab2), (part_h, first)
    )
    wait_all(copies[:3])
    left = hidden_terms(saved[...], mixed[...], slab)
    wait_all(copies[3:])
    left2 = hidden_terms(saved[...], mixed[...], slab2)
    for c in range(0, out.shape[1], COLS):
        cut = slice(c, c + COLS)
        part = first[:, cut] + jnp.dot(left, slab[:, cut], preferred_element_type=f32)
        part = part + jnp.dot(left2, slab2[:, cut], preferred_element_type=f32)
        out[:, cut] = part.astype(bf16)


def placed(select_t, rows):
    high = rows.astype(bf16)
    rest = rows - high.astype(f32)
    mid = rest.astype(bf16)
    low = (rest - mid.astype(f32)).astype(bf16)
    return sum(jnp.dot(select_t, p, preferred_element_type=f32) for p in (low, mid, high))


def combine_body(
    parts, columns_h, rows16_h, picked_h, gain_h, x_in, upstream, fwd_out, bwd_out,
    columns, rows16, picked, gain, sems,
):
    wait_all(
        started(
            sems, (columns_h, columns), (rows16_h, rows16), (picked_h, picked), (gain_h, gain)
        )
    )
    half = parts.shape[0] // EXP_WIN

    def summed(start):
        return jnp.concatenate(
            [
                sum(
                    parts[e * half + i, start : start + CAP, :].astype(f32) for i in range(half)
                )
                for e in range(EXP_WIN)
            ],
            axis=0,
        )

    rows = summed(0) * rows16[1, :, 0:1]
    fwd_out[...] = (x_in[...].astype(f32) + placed(columns[1, :, :], rows)).astype(bf16)
    weighted = gain[...].astype(f32) * summed(CAP)
    inv = rows16[2, :, 0:1]
    x = picked[...].astype(f32)
    rows = inv * weighted - x * (inv * inv * inv) * jnp.mean(x * weighted, axis=1, keepdims=True)
    bwd_out[...] = (upstream[...].astype(f32) + placed(columns[0, :, :], rows)).astype(bf16)


def shifted(block, axis, distance):
    n = lax.axis_size(axis)
    return lax.ppermute(block, axis, [((i - distance) % n, i) for i in range(n)])


def over_y(block):
    return lax.all_to_all(block, "y", split_axis=0, concat_axis=0, tiled=True)


def body(
    fwd_sent, bwd_sent, bwd_saved, fwd_routes, bwd_routes, fwd_logits, bwd_logits,
    norm_gain, w_gate, w_up, w_down,
):
    stops = lax.axis_size("y")
    tokens, width = fwd_sent.shape[1:]
    dma = pltpu.SemaphoreType.DMA
    upstream = shifted(bwd_sent[0], "section", -1)
    x_in = shifted(fwd_sent[0], "section", 1)
    slab = jnp.concatenate([w_gate[0].T, w_up[0].T, w_down[0]], axis=0)
    slab_core = shifted(slab, "core", 1)
    slab_x = shifted(slab, "xl", 1)
    saved_send, picked, columns, rows16, usage = kernel_call(
        prepare_body,
        (in_hbm((stops, CAP, width), bf16), in_hbm((SLOTS, width), bf16),
         in_hbm((EXP_WIN, tokens, SLOTS), bf16), in_hbm((3, SLOTS, EXPERTS), f32),
         in_hbm((2, EXPERTS), f32)),
        [HBM] * 6, [VMEM] * 5,
        [pltpu.VMEM((tokens, width), bf16), pltpu.VMEM((1, width), bf16),
         pltpu.VMEM((TOPK, tokens), jnp.int32), pltpu.VMEM((tokens, EXPERTS), f32),
         pltpu.VMEM((TOPK, tokens), jnp.int32), pltpu.VMEM((tokens, EXPERTS), f32), dma((6,))],
        bwd_saved[0], norm_gain, bwd_routes[0].T, bwd_logits[0], fwd_routes[0].T, fwd_logits[0],
    )
    devices = lax.axis_size(EXPERT_AXES)
    shared = lax.all_to_all(
        jnp.broadcast_to(usage[None], (devices, 2, EXPERTS)),
        EXPERT_AXES, split_axis=0, concat_axis=0, tiled=True,
    )
    saved_send, shared = lax.optimization_barrier((saved_send, shared))
    saved_all = over_y(saved_send).reshape(-1, width)
    mixed_send = kernel_call(
        rows_body, in_hbm((stops, 2 * CAP, width), bf16), [VMEM, VMEM, HBM, HBM, HBM], VMEM,
        [pltpu.VMEM((EXP_WIN, tokens, SLOTS), bf16), pltpu.VMEM((SLOTS, EXPERTS), f32),
         pltpu.VMEM((1, width), bf16), dma((3,))],
        x_in, upstream, columns, rows16, norm_gain,
    )
    mixed_all = over_y(mixed_send).reshape(-1, width)
    loads = [pltpu.VMEM(v.shape, bf16) for v in (saved_all, mixed_all, slab, slab)]
    first = kernel_call(
        expert_first_body, in_hbm(mixed_all.shape, f32), [HBM] * 4, VMEM, loads + [dma((4,))],
        saved_all, mixed_all, slab, slab_core,
    )
    slab_x, first = lax.optimization_barrier((slab_x, first))
    slab_x_core = shifted(slab_x, "core", 1)
    result = kernel_call(
        expert_second_body, in_hbm(mixed_all.shape, bf16), [HBM] * 5, VMEM,
        loads + [pltpu.VMEM(first.shape, f32), dma((5,))],
        saved_all, mixed_all, slab_x, slab_x_core, first,
    )
    parts = over_y(result.reshape(stops, 2 * CAP, width))
    full = in_hbm((tokens, width), bf16)
    fwd_out, bwd_out = kernel_call(
        combine_body, (full, full), [VMEM] + [HBM] * 4 + [VMEM] * 2, [VMEM] * 2,
        [pltpu.VMEM(columns.shape, bf16),
         pltpu.VMEM(rows16.shape, f32), pltpu.VMEM(picked.shape, bf16),
         pltpu.VMEM((1, width), bf16), dma((4,))],
        parts, columns, rows16, picked, norm_gain, x_in, upstream,
    )
    counts, prob_sums = jnp.sum(shared, axis=0)
    tokens_all = tokens * devices
    balance = EXPERTS * (counts / (tokens_all * TOPK)) * (prob_sums / tokens_all)
    return (fwd_out[None], bwd_out[None], balance[None])


def solution(mesh):
    sections = mesh.shape["section"]
    grid = mesh.devices.reshape(sections, -1, 2, 2)
    inner = Mesh(grid, ("section",) + EXPERT_AXES)
    rows = P("section", EXPERT_AXES, None)
    return jax.shard_map(
        body,
        mesh=inner,
        in_specs=(
            rows, rows, rows, rows, rows, rows, rows,
            P("section", None),
            P("section", None, EXPERT_AXES),
            P("section", None, EXPERT_AXES),
            rows,
        ),
        out_specs=(rows, rows, P("section", None)),
        check_vma=False,
    )
```

```python
import jax
import jax.numpy as jnp
from jax import lax
from jax.experimental import pallas as pl
from jax.experimental.pallas import tpu as pltpu
from jax.sharding import Mesh, PartitionSpec as P

EXPERTS = 128
TOPK = 8
EXP_WIN = 2
CAP = 8
SLOTS = EXP_WIN * CAP
EPS = 1e-06
exact = lax.Precision.HIGHEST
f32 = jnp.float32
bf16 = jnp.bfloat16
NT = (((1,), (1,)), ((), ()))
PARAMS = pltpu.CompilerParams(vmem_limit_bytes=48 << 20)
EXPERT_AXES = ("y", "xl", "core")


def shape(dims, dtype):
    return jax.ShapeDtypeStruct(dims, dtype)


def iota(dims, axis):
    return lax.broadcasted_iota(jnp.int32, dims, axis)


def hot_columns(routes_t, experts):
    ids = iota((experts, routes_t.shape[1]), 0)
    hot_t = jnp.zeros(ids.shape, f32)
    for k in range(TOPK):
        hot_t = hot_t + jnp.where(ids == routes_t[k : k + 1, :], 1.0, 0.0)
    return hot_t


def selection(hot_t):
    tokens = hot_t.shape[1]
    first = hot_t[0:8, :]
    before = jnp.where(iota((tokens, tokens), 0) < iota((tokens, tokens), 1), 1.0, 0.0)
    earlier = jnp.dot(first.astype(bf16), before.astype(bf16), preferred_element_type=f32)
    slot = iota((CAP, tokens), 0).astype(f32)
    return jnp.concatenate(
        [
            jnp.where((earlier[e : e + 1, :] == slot) & (first[e : e + 1, :] > 0.5), 1.0, 0.0)
            for e in range(EXP_WIN)
        ],
        axis=0,
    ).astype(bf16)


def slot_tables(routes_t, logits):
    tokens, experts = logits.shape
    hot_t = hot_columns(routes_t, experts)
    eye = jnp.where(iota((tokens, tokens), 0) == iota((tokens, tokens), 1), 1.0, 0.0).astype(bf16)
    hot = lax.dot_general(eye, hot_t.astype(bf16), NT, preferred_element_type=f32)
    chosen = jnp.where(hot > 0.5, logits, -jnp.inf)
    powers = jnp.exp(chosen - jnp.max(chosen, axis=1, keepdims=True))
    gates = powers / jnp.sum(powers, axis=1, keepdims=True)
    select = selection(hot_t)
    select_t = lax.dot_general(eye, select, NT, preferred_element_type=f32)
    picked = jnp.dot(select.astype(f32), gates, precision=exact, preferred_element_type=f32)
    own = iota((SLOTS, experts), 1) == iota((SLOTS, experts), 0) // CAP
    gate_slot = jnp.sum(jnp.where(own, picked, 0.0), axis=1, keepdims=True)
    return hot, select, select_t.astype(bf16), gate_slot


HBM = pl.BlockSpec(memory_space=pltpu.HBM)
VMEM = pl.BlockSpec(memory_space=pltpu.VMEM)


def in_hbm(dims, dtype):
    return pltpu.HBM(dims, dtype)


def kernel_call(body, outs, in_specs, out_specs, scratch, *args):
    args = [
        pltpu.with_memory_space_constraint(v, pltpu.HBM) if spec is HBM else v
        for v, spec in zip(args, in_specs)
    ]
    return pl.pallas_call(
        body, out_shape=outs, in_specs=in_specs, out_specs=out_specs, scratch_shapes=scratch,
        compiler_params=PARAMS,
    )(*args)


def started(sems, *pairs):
    copies = [pltpu.make_async_copy(src, dst, sems.at[i]) for i, (src, dst) in enumerate(pairs)]
    for copy in copies:
        copy.start()
    return copies


def wait_all(copies):
    for copy in copies:
        copy.wait()


def normed_rows(rows, gain):
    inverse = lax.rsqrt(jnp.mean(rows * rows, axis=1, keepdims=True) + EPS)
    return (rows * inverse * gain).astype(bf16), inverse


def by_expert(stops):
    return [(i, i * EXP_WIN // stops * CAP) for i in range(stops)]


def prepare_body(
    saved_h, gain_h, broutes_h, blogits_h, froutes_h, flogits_h,
    send, picked, columns, rows16, usage,
    saved, gain, broutes, blogits, froutes, flogits, sems,
):
    copies = started(
        sems, (broutes_h, broutes), (blogits_h, blogits), (froutes_h, froutes),
        (flogits_h, flogits), (gain_h, gain), (saved_h, saved),
    )
    wait_all(copies[:4])
    _, select, bselect_t, bgate = slot_tables(broutes[...], blogits[...])
    logits = flogits[...]
    hot, _, fselect_t, fgate = slot_tables(froutes[...], logits)
    powers = jnp.exp(logits - jnp.max(logits, axis=1, keepdims=True))
    probs = powers / jnp.sum(powers, axis=1, keepdims=True)
    usage[...] = jnp.concatenate(
        [jnp.sum(hot, axis=0, keepdims=True), jnp.sum(probs, axis=0, keepdims=True)], axis=0
    )
    wait_all(copies[4:])
    rows = jnp.dot(select, saved[...], preferred_element_type=f32)
    normed, inverse = normed_rows(rows, gain[...].astype(f32))
    picked[...] = rows.astype(bf16)
    columns[0, :, :] = bselect_t
    columns[1, :, :] = fselect_t
    wide = (SLOTS, EXPERTS)
    rows16[0, :, :] = jnp.broadcast_to(bgate, wide)
    rows16[1, :, :] = jnp.broadcast_to(fgate, wide)
    rows16[2, :, :] = jnp.broadcast_to(inverse, wide)
    for i, r in by_expert(send.shape[0]):
        send[i, :, :] = normed[r : r + CAP, :]


def pick_body(froutes_h, broutes_h, ahead_h, behind_h, fpicked, bpicked, froutes, broutes, ahead, behind, sems):
    copies = started(
        sems, (froutes_h, froutes), (broutes_h, broutes), (ahead_h, ahead), (behind_h, behind)
    )
    wait_all(copies[:2])
    fselect = selection(hot_columns(froutes[...], EXPERTS))
    bselect = selection(hot_columns(broutes[...], EXPERTS))
    wait_all(copies[2:])
    fpicked[...] = jnp.dot(fselect, ahead[...], preferred_element_type=f32).astype(bf16)
    bpicked[...] = jnp.dot(bselect, behind[...], preferred_element_type=f32).astype(bf16)


def rows_body(fpicked, bpicked, rows16_h, gain_h, send, gates, gain, sems):
    copies = started(sems, (rows16_h.at[0], gates), (gain_h, gain))
    wait_all(copies)
    normed = normed_rows(fpicked[...].astype(f32), gain[...].astype(f32))[0]
    grads = (bpicked[...].astype(f32) * gates[:, 0:1]).astype(bf16)
    for i, r in by_expert(send.shape[0]):
        send[i, 0:CAP, :] = normed[r : r + CAP, :]
        send[i, CAP : 2 * CAP, :] = grads[r : r + CAP, :]


COLS = 512


def nt(a, b):
    return lax.dot_general(a, b, NT, preferred_element_type=f32)


def hidden_terms(saved, mixed, slab):
    hid = slab.shape[0] // 3
    kept = nt(saved, slab[0 : 2 * hid, :])
    pre = nt(mixed, slab[...]).reshape(-1, 2 * CAP, 3 * hid)
    forward, grads = pre[:, 0:CAP, :], pre[:, CAP:, :]
    h = jax.nn.silu(forward[:, :, :hid]) * forward[:, :, hid : 2 * hid]
    kept = kept.reshape(-1, CAP, 2 * hid)
    a, b, d_hidden = kept[:, :, :hid], kept[:, :, hid:], grads[:, :, 2 * hid :]
    sigma = jax.nn.sigmoid(a)
    d_gate = d_hidden * b * sigma * (1.0 + a * (1.0 - sigma))
    d_up = d_hidden * a * sigma
    none = jnp.zeros_like(h)
    top = jnp.concatenate([none, none, h], axis=2)
    low = jnp.concatenate([d_gate, d_up, none], axis=2)
    return jnp.concatenate([top, low], axis=1).reshape(-1, 3 * hid).astype(bf16)


def expert_first_body(saved_h, mixed_h, slab_h, slab2_h, out, saved, mixed, slab, slab2, sems):
    copies = started(
        sems, (saved_h, saved), (mixed_h, mixed), (slab_h, slab), (slab2_h, slab2)
    )
    wait_all(copies[:3])
    left = hidden_terms(saved[...], mixed[...], slab)
    copies[3].wait()
    left2 = hidden_terms(saved[...], mixed[...], slab2)
    for c in range(0, out.shape[1], COLS):
        cut = slice(c, c + COLS)
        part = jnp.dot(left, slab[:, cut], preferred_element_type=f32)
        out[:, cut] = part + jnp.dot(left2, slab2[:, cut], preferred_element_type=f32)


def expert_second_body(
    saved_h, mixed_h, slab_h, slab2, part_h, out, saved, mixed, slab, first, sems
):
    copies = started(
        sems, (saved_h, saved), (mixed_h, mixed), (slab_h, slab), (part_h, first)
    )
    wait_all(copies[:3])
    left = hidden_terms(saved[...], mixed[...], slab)
    left2 = hidden_terms(saved[...], mixed[...], slab2)
    copies[3].wait()
    for c in range(0, out.shape[1], COLS):
        cut = slice(c, c + COLS)
        part = first[:, cut] + jnp.dot(left, slab[:, cut], preferred_element_type=f32)
        part = part + jnp.dot(left2, slab2[:, cut], preferred_element_type=f32)
        out[:, cut] = part.astype(bf16)


def placed(select_t, rows):
    high = rows.astype(bf16)
    rest = rows - high.astype(f32)
    mid = rest.astype(bf16)
    low = (rest - mid.astype(f32)).astype(bf16)
    return sum(jnp.dot(select_t, p, preferred_element_type=f32) for p in (low, mid, high))


def combine_body(
    parts, columns_h, rows16_h, picked_h, gain_h, x_in, upstream, fwd_out, bwd_out,
    columns, rows16, picked, gain, sems,
):
    wait_all(
        started(
            sems, (columns_h, columns), (rows16_h, rows16), (picked_h, picked), (gain_h, gain)
        )
    )
    half = parts.shape[0] // EXP_WIN

    def summed(start):
        return jnp.concatenate(
            [
                sum(
                    parts[e * half + i, start : start + CAP, :].astype(f32) for i in range(half)
                )
                for e in range(EXP_WIN)
            ],
            axis=0,
        )

    rows = summed(0) * rows16[1, :, 0:1]
    fwd_out[...] = (x_in[...].astype(f32) + placed(columns[1, :, :], rows)).astype(bf16)
    weighted = gain[...].astype(f32) * summed(CAP)
    inv = rows16[2, :, 0:1]
    x = picked[...].astype(f32)
    rows = inv * weighted - x * (inv * inv * inv) * jnp.mean(x * weighted, axis=1, keepdims=True)
    bwd_out[...] = (upstream[...].astype(f32) + placed(columns[0, :, :], rows)).astype(bf16)


def shifted(block, axis, distance):
    n = lax.axis_size(axis)
    return lax.ppermute(block, axis, [((i - distance) % n, i) for i in range(n)])


def summed_over(value, axes):
    for axis in axes:
        n, step = lax.axis_size(axis), 1
        while step < n:
            value = value + lax.ppermute(value, axis, [(i, i ^ step) for i in range(n)])
            step *= 2
    return value


def over_y(block):
    return lax.all_to_all(block, "y", split_axis=0, concat_axis=0, tiled=True)


def body(
    fwd_sent, bwd_sent, bwd_saved, fwd_routes, bwd_routes, fwd_logits, bwd_logits,
    norm_gain, w_gate, w_up, w_down,
):
    stops = lax.axis_size("y")
    tokens, width = fwd_sent.shape[1:]
    dma = pltpu.SemaphoreType.DMA
    fwd_routes_t, bwd_routes_t = fwd_routes[0].T, bwd_routes[0].T
    froutes_next = shifted(fwd_routes_t, "section", -1)
    broutes_last = shifted(bwd_routes_t, "section", 1)
    slab = jnp.concatenate([w_gate[0].T, w_up[0].T, w_down[0]], axis=0)
    slab_core = shifted(slab, "core", 1)
    slab_x = shifted(slab, "xl", 1)
    saved_send, picked, columns, rows16, usage = kernel_call(
        prepare_body,
        (in_hbm((stops, CAP, width), bf16), in_hbm((SLOTS, width), bf16),
         in_hbm((EXP_WIN, tokens, SLOTS), bf16), in_hbm((3, SLOTS, EXPERTS), f32),
         in_hbm((2, EXPERTS), f32)),
        [HBM] * 6, [VMEM] * 5,
        [pltpu.VMEM((tokens, width), bf16), pltpu.VMEM((1, width), bf16),
         pltpu.VMEM((TOPK, tokens), jnp.int32), pltpu.VMEM((tokens, EXPERTS), f32),
         pltpu.VMEM((TOPK, tokens), jnp.int32), pltpu.VMEM((tokens, EXPERTS), f32), dma((6,))],
        bwd_saved[0], norm_gain, bwd_routes_t, bwd_logits[0], fwd_routes_t, fwd_logits[0],
    )
    saved_all = over_y(saved_send).reshape(-1, width)
    routes_shape = pltpu.VMEM((TOPK, tokens), jnp.int32)
    block = pltpu.VMEM((tokens, width), bf16)
    slot_rows = in_hbm((SLOTS, width), bf16)
    fpicked, bpicked = kernel_call(
        pick_body, (slot_rows, slot_rows), [HBM] * 4, [VMEM] * 2,
        [routes_shape, routes_shape, block, block, dma((4,))],
        froutes_next, broutes_last, fwd_sent[0], bwd_sent[0],
    )
    fpicked = shifted(fpicked, "section", 1)
    bpicked = shifted(bpicked, "section", -1)
    mixed_send = kernel_call(
        rows_body, in_hbm((stops, 2 * CAP, width), bf16), [VMEM, VMEM, HBM, HBM], VMEM,
        [pltpu.VMEM((SLOTS, EXPERTS), f32), pltpu.VMEM((1, width), bf16), dma((2,))],
        fpicked, bpicked, rows16, norm_gain,
    )
    mixed_all = over_y(mixed_send).reshape(-1, width)
    loads = [pltpu.VMEM(v.shape, bf16) for v in (saved_all, mixed_all, slab, slab)]
    first = kernel_call(
        expert_first_body, in_hbm(mixed_all.shape, f32), [HBM] * 4, VMEM, loads + [dma((4,))],
        saved_all, mixed_all, slab, slab_core,
    )
    slab_x, first, fwd_block, bwd_block = lax.optimization_barrier(
        (slab_x, first, fwd_sent[0], bwd_sent[0])
    )
    slab_x_core = shifted(slab_x, "core", 1)
    upstream = shifted(bwd_block, "section", -1)
    x_in = shifted(fwd_block, "section", 1)
    result = kernel_call(
        expert_second_body, in_hbm(mixed_all.shape, bf16), [HBM, HBM, HBM, VMEM, HBM], VMEM,
        loads[:3] + [pltpu.VMEM(first.shape, f32), dma((4,))],
        saved_all, mixed_all, slab_x, slab_x_core, first,
    )
    result, usage = lax.optimization_barrier((result, usage))
    parts = over_y(result.reshape(stops, 2 * CAP, width))
    full = in_hbm((tokens, width), bf16)
    fwd_out, bwd_out = kernel_call(
        combine_body, (full, full), [VMEM] + [HBM] * 4 + [VMEM] * 2, [VMEM] * 2,
        [pltpu.VMEM(columns.shape, bf16),
         pltpu.VMEM(rows16.shape, f32), pltpu.VMEM(picked.shape, bf16),
         pltpu.VMEM((1, width), bf16), dma((4,))],
        parts, columns, rows16, picked, norm_gain, x_in, upstream,
    )
    counts, prob_sums = summed_over(usage, EXPERT_AXES)
    tokens_all = tokens * lax.axis_size(EXPERT_AXES)
    balance = EXPERTS * (counts / (tokens_all * TOPK)) * (prob_sums / tokens_all)
    return (fwd_out[None], bwd_out[None], balance[None])


def solution(mesh):
    sections = mesh.shape["section"]
    grid = mesh.devices.reshape(sections, -1, 2, 2)
    inner = Mesh(grid, ("section",) + EXPERT_AXES)
    rows = P("section", EXPERT_AXES, None)
    return jax.shard_map(
        body,
        mesh=inner,
        in_specs=(
            rows, rows, rows, rows, rows, rows, rows,
            P("section", None),
            P("section", None, EXPERT_AXES),
            P("section", None, EXPERT_AXES),
            rows,
        ),
        out_specs=(rows, rows, P("section", None)),
        check_vma=False,
    )
```

```python
import jax
import jax.numpy as jnp
from jax import lax
from jax.experimental import pallas as pl
from jax.experimental.pallas import tpu as pltpu
from jax.sharding import Mesh, PartitionSpec as P

EXPERTS = 128
TOPK = 8
EXP_WIN = 2
CAP = 8
SLOTS = EXP_WIN * CAP
EPS = 1e-06
exact = lax.Precision.HIGHEST
f32 = jnp.float32
bf16 = jnp.bfloat16
NT = (((1,), (1,)), ((), ()))
PARAMS = pltpu.CompilerParams(vmem_limit_bytes=48 << 20)
EXPERT_AXES = ("y", "xl", "core")


def shape(dims, dtype):
    return jax.ShapeDtypeStruct(dims, dtype)


def iota(dims, axis):
    return lax.broadcasted_iota(jnp.int32, dims, axis)


def hot_columns(routes_t, experts):
    ids = iota((experts, routes_t.shape[1]), 0)
    hot_t = jnp.zeros(ids.shape, f32)
    for k in range(TOPK):
        hot_t = hot_t + jnp.where(ids == routes_t[k : k + 1, :], 1.0, 0.0)
    return hot_t


def selection(hot_t):
    tokens = hot_t.shape[1]
    first = hot_t[0:8, :]
    before = jnp.where(iota((tokens, tokens), 0) < iota((tokens, tokens), 1), 1.0, 0.0)
    earlier = jnp.dot(first.astype(bf16), before.astype(bf16), preferred_element_type=f32)
    slot = iota((CAP, tokens), 0).astype(f32)
    return jnp.concatenate(
        [
            jnp.where((earlier[e : e + 1, :] == slot) & (first[e : e + 1, :] > 0.5), 1.0, 0.0)
            for e in range(EXP_WIN)
        ],
        axis=0,
    ).astype(bf16)


def slot_tables(routes_t, logits):
    tokens, experts = logits.shape
    hot_t = hot_columns(routes_t, experts)
    eye = jnp.where(iota((tokens, tokens), 0) == iota((tokens, tokens), 1), 1.0, 0.0).astype(bf16)
    hot = lax.dot_general(eye, hot_t.astype(bf16), NT, preferred_element_type=f32)
    chosen = jnp.where(hot > 0.5, logits, -jnp.inf)
    powers = jnp.exp(chosen - jnp.max(chosen, axis=1, keepdims=True))
    gates = powers / jnp.sum(powers, axis=1, keepdims=True)
    select = selection(hot_t)
    select_t = lax.dot_general(eye, select, NT, preferred_element_type=f32)
    picked = jnp.dot(select.astype(f32), gates, precision=exact, preferred_element_type=f32)
    own = iota((SLOTS, experts), 1) == iota((SLOTS, experts), 0) // CAP
    gate_slot = jnp.sum(jnp.where(own, picked, 0.0), axis=1, keepdims=True)
    return hot, select, select_t.astype(bf16), gate_slot


HBM = pl.BlockSpec(memory_space=pltpu.HBM)
VMEM = pl.BlockSpec(memory_space=pltpu.VMEM)


def in_hbm(dims, dtype):
    return pltpu.HBM(dims, dtype)


def kernel_call(body, outs, in_specs, out_specs, scratch, *args):
    args = [
        pltpu.with_memory_space_constraint(v, pltpu.HBM) if spec is HBM else v
        for v, spec in zip(args, in_specs)
    ]
    return pl.pallas_call(
        body, out_shape=outs, in_specs=in_specs, out_specs=out_specs, scratch_shapes=scratch,
        compiler_params=PARAMS,
    )(*args)


def started(sems, *pairs):
    copies = [pltpu.make_async_copy(src, dst, sems.at[i]) for i, (src, dst) in enumerate(pairs)]
    for copy in copies:
        copy.start()
    return copies


def wait_all(copies):
    for copy in copies:
        copy.wait()


def in_parts(value):
    high = value.astype(bf16)
    rest = value - high.astype(f32)
    mid = rest.astype(bf16)
    return (rest - mid.astype(f32)).astype(bf16), mid, high


def normed_rows(rows, gain):
    inverse = lax.rsqrt(jnp.mean(rows * rows, axis=1, keepdims=True) + EPS)
    return (rows * inverse * gain).astype(bf16), inverse


def by_expert(stops):
    return [(i, i * EXP_WIN // stops * CAP) for i in range(stops)]


def prepare_body(
    saved_h, gain_h, broutes_h, blogits_h, froutes_h, flogits_h,
    send, picked, columns, rows16,
    saved, gain, broutes, blogits, froutes, flogits, sems,
):
    copies = started(
        sems, (broutes_h, broutes), (blogits_h, blogits), (froutes_h, froutes),
        (flogits_h, flogits), (gain_h, gain), (saved_h, saved),
    )
    wait_all(copies[:4])
    _, select, bselect_t, bgate = slot_tables(broutes[...], blogits[...])
    logits = flogits[...]
    hot, _, fselect_t, fgate = slot_tables(froutes[...], logits)
    powers = jnp.exp(logits - jnp.max(logits, axis=1, keepdims=True))
    probs = powers / jnp.sum(powers, axis=1, keepdims=True)
    usage = [jnp.sum(hot, axis=0, keepdims=True)]
    usage += [p.astype(f32) for p in in_parts(jnp.sum(probs, axis=0, keepdims=True))]
    usage += [jnp.zeros((CAP - len(usage), EXPERTS), f32)]
    usage = jnp.concatenate(usage, axis=0).astype(bf16)
    width = saved.shape[1]
    wait_all(copies[4:])
    rows = jnp.dot(select, saved[...], preferred_element_type=f32)
    normed, inverse = normed_rows(rows, gain[...].astype(f32))
    picked[...] = rows.astype(bf16)
    columns[0, :, :] = bselect_t
    columns[1, :, :] = fselect_t
    wide = (SLOTS, EXPERTS)
    rows16[0, :, :] = jnp.broadcast_to(bgate, wide)
    rows16[1, :, :] = jnp.broadcast_to(fgate, wide)
    rows16[2, :, :] = jnp.broadcast_to(inverse, wide)
    for i, r in by_expert(send.shape[0]):
        send[i, :, 0:width] = normed[r : r + CAP, :]
        send[i, :, width:] = usage


def rows_body(x_in, upstream, columns_h, rows16_h, gain_h, send, columns, gates, gain, sems):
    copies = started(sems, (columns_h, columns), (rows16_h.at[0], gates), (gain_h, gain))
    copies[0].wait()

    def chosen(i, block):
        return lax.dot_general(
            columns[i, :, :], block[...], (((0,), (0,)), ((), ())), preferred_element_type=f32
        )

    rows = chosen(1, x_in)
    grads = chosen(0, upstream)
    wait_all(copies[1:])
    normed = normed_rows(rows, gain[...].astype(f32))[0]
    grads = (grads * gates[:, 0:1]).astype(bf16)
    for i, r in by_expert(send.shape[0]):
        send[i, 0:CAP, :] = normed[r : r + CAP, :]
        send[i, CAP : 2 * CAP, :] = grads[r : r + CAP, :]


COLS = 512


def nt(a, b):
    return lax.dot_general(a, b, NT, preferred_element_type=f32)


def row_blocks(mixed_h, start, dst):
    return [
        (mixed_h.at[i, start : start + CAP, :], dst.at[i * CAP : (i + 1) * CAP, :])
        for i in range(mixed_h.shape[0])
    ]


def stacked(dst, *blocks):
    pairs, row = [], 0
    for block in blocks:
        pairs.append((block, dst.at[row : row + block.shape[0], :]))
        row += block.shape[0]
    return pairs


def hidden_of(pre):
    half, hid = pre.shape[0] // 2, pre.shape[1] // 2
    a, b = pre[:half, :hid], pre[:half, hid:]
    return (jax.nn.silu(a) * b).astype(bf16), pre[half:, :hid], pre[half:, hid:]


def hidden_grads(a, b, d_hidden):
    sigma = jax.nn.sigmoid(a)
    d_gate = d_hidden * b * sigma * (1.0 + a * (1.0 - sigma))
    d_up = d_hidden * a * sigma
    return jnp.concatenate([d_gate, d_up], axis=1).astype(bf16)


def slab_pairs(slabs, gu, down):
    hid = down.shape[0] // len(slabs)
    pieces = [w.at[m * hid : (m + 1) * hid, :] for m in range(3) for w in slabs]
    gates = len(slabs) * 2
    return stacked(gu, *pieces[:gates]), stacked(down, *pieces[gates:])


def expert_own_body(
    mixed_h, saved_h, slab0, slab1, first, usage, both, grads, tail, gu, down, sems
):
    rows, width = both.shape
    gates, downs = slab_pairs((slab0, slab1), gu, down)
    pairs = row_blocks(mixed_h, 0, both) + gates
    pairs.append((saved_h.at[:, 0:width], both.at[rows // 2 :, :]))
    early = len(pairs)
    pairs += row_blocks(mixed_h, CAP, grads) + downs
    pairs.append((saved_h.at[:, width:], tail))
    copies = started(sems, *pairs)
    wait_all(copies[:early])
    h, a, b = hidden_of(nt(both[...], gu[...]))
    wait_all(copies[early:])
    terms = hidden_grads(a, b, nt(grads[...], down[...]))
    for c in range(0, width, COLS):
        cut = slice(c, c + COLS)
        first[0, :, cut] = jnp.dot(h, down[:, cut], preferred_element_type=f32)
        first[1, :, cut] = jnp.dot(terms, gu[:, cut], preferred_element_type=f32)
    shares = sum(
        tail[i * CAP : (i + 1) * CAP, :].astype(f32) for i in range(mixed_h.shape[0])
    )
    usage[...] = jnp.concatenate(
        [shares[0:1, :], shares[1:2, :] + shares[2:3, :] + shares[3:4, :]], axis=0
    )


def expert_beside_body(
    mixed_h, saved_h, first_h, slab0, slab1, out, both, grads, first, gu, down, sems
):
    rows, width = both.shape
    gates, downs = slab_pairs((slab0, slab1), gu, down)
    pairs = row_blocks(mixed_h, 0, both) + gates
    pairs.append((saved_h.at[:, 0:width], both.at[rows // 2 :, :]))
    early = len(pairs)
    copies = started(sems, *pairs, *row_blocks(mixed_h, CAP, grads), *downs, (first_h, first))
    wait_all(copies[:early])
    h, a, b = hidden_of(nt(both[...], gu[...]))
    wait_all(copies[early:])
    terms = hidden_grads(a, b, nt(grads[...], down[...]))
    for c in range(0, width, COLS):
        cut = slice(c, c + COLS)
        fwd = first[0, :, cut] + jnp.dot(h, down[:, cut], preferred_element_type=f32)
        bwd = first[1, :, cut] + jnp.dot(terms, gu[:, cut], preferred_element_type=f32)
        for i in range(out.shape[0]):
            out[i, 0:CAP, cut] = fwd[i * CAP : (i + 1) * CAP, :].astype(bf16)
            out[i, CAP : 2 * CAP, cut] = bwd[i * CAP : (i + 1) * CAP, :].astype(bf16)


def placed(select_t, rows):
    return sum(jnp.dot(select_t, p, preferred_element_type=f32) for p in in_parts(rows))


def combine_body(
    parts, columns_h, rows16_h, picked_h, gain_h, x_in, upstream, fwd_out, bwd_out,
    columns, rows16, picked, gain, sems,
):
    wait_all(
        started(
            sems, (columns_h, columns), (rows16_h, rows16), (picked_h, picked), (gain_h, gain)
        )
    )
    half = parts.shape[0] // EXP_WIN

    def summed(start):
        return jnp.concatenate(
            [
                sum(
                    parts[e * half + i, start : start + CAP, :].astype(f32) for i in range(half)
                )
                for e in range(EXP_WIN)
            ],
            axis=0,
        )

    rows = summed(0) * rows16[1, :, 0:1]
    fwd_out[...] = (x_in[...].astype(f32) + placed(columns[1, :, :], rows)).astype(bf16)
    weighted = gain[...].astype(f32) * summed(CAP)
    inv = rows16[2, :, 0:1]
    x = picked[...].astype(f32)
    rows = inv * weighted - x * (inv * inv * inv) * jnp.mean(x * weighted, axis=1, keepdims=True)
    bwd_out[...] = (upstream[...].astype(f32) + placed(columns[0, :, :], rows)).astype(bf16)


def shifted(block, axis, distance):
    n = lax.axis_size(axis)
    return lax.ppermute(block, axis, [((i - distance) % n, i) for i in range(n)])


def over_y(block):
    return lax.all_to_all(block, "y", split_axis=0, concat_axis=0, tiled=True)


def body(
    fwd_sent, bwd_sent, bwd_saved, fwd_routes, bwd_routes, fwd_logits, bwd_logits,
    norm_gain, w_gate, w_up, w_down,
):
    stops = lax.axis_size("y")
    tokens, width = fwd_sent.shape[1:]
    dma = pltpu.SemaphoreType.DMA
    upstream = shifted(bwd_sent[0], "section", -1)
    x_in = shifted(fwd_sent[0], "section", 1)
    slab = jnp.concatenate([w_gate[0].T, w_up[0].T, w_down[0]], axis=0)
    slab_x = shifted(slab, "xl", 1)
    slab_core = shifted(slab, "core", 1)
    saved_send, picked, columns, rows16 = kernel_call(
        prepare_body,
        (in_hbm((stops, CAP, width + EXPERTS), bf16), in_hbm((SLOTS, width), bf16),
         in_hbm((EXP_WIN, tokens, SLOTS), bf16), in_hbm((3, SLOTS, EXPERTS), f32)),
        [HBM] * 6, [VMEM] * 4,
        [pltpu.VMEM((tokens, width), bf16), pltpu.VMEM((1, width), bf16),
         pltpu.VMEM((TOPK, tokens), jnp.int32), pltpu.VMEM((tokens, EXPERTS), f32),
         pltpu.VMEM((TOPK, tokens), jnp.int32), pltpu.VMEM((tokens, EXPERTS), f32), dma((6,))],
        bwd_saved[0], norm_gain, bwd_routes[0].T, bwd_logits[0], fwd_routes[0].T, fwd_logits[0],
    )
    saved_all = over_y(saved_send).reshape(-1, width + EXPERTS)
    mixed_send = kernel_call(
        rows_body, in_hbm((stops, 2 * CAP, width), bf16), [VMEM, VMEM, HBM, HBM, HBM], VMEM,
        [pltpu.VMEM((EXP_WIN, tokens, SLOTS), bf16), pltpu.VMEM((SLOTS, EXPERTS), f32),
         pltpu.VMEM((1, width), bf16), dma((3,))],
        x_in, upstream, columns, rows16, norm_gain,
    )
    mixed_all = over_y(mixed_send)
    count, hid = stops * CAP, slab.shape[0] // 3
    vmem = pltpu.VMEM
    both, grads = vmem((2 * count, width), bf16), vmem((count, width), bf16)
    gu, down = vmem((4 * hid, width), bf16), vmem((2 * hid, width), bf16)
    sums = in_hbm((2, count, width), f32)
    first, usage = kernel_call(
        expert_own_body, (sums, in_hbm((2, EXPERTS), f32)), [HBM] * 4, [VMEM] * 2,
        [both, grads, vmem((count, EXPERTS), bf16), gu, down, dma((2 * stops + 8,))],
        mixed_all, saved_all, slab, slab_core,
    )
    slab_x, first = lax.optimization_barrier((slab_x, first))
    result = kernel_call(
        expert_beside_body, in_hbm((stops, 2 * CAP, width), bf16), [HBM] * 4 + [VMEM], VMEM,
        [both, grads, vmem(sums.shape, f32), gu, down, dma((2 * stops + 8,))],
        mixed_all, saved_all, first, slab_x, shifted(slab_x, "core", 1),
    )
    result, usage = lax.optimization_barrier((result, usage))
    parts = over_y(result)
    full = in_hbm((tokens, width), bf16)
    fwd_out, bwd_out = kernel_call(
        combine_body, (full, full), [VMEM] + [HBM] * 4 + [VMEM] * 2, [VMEM] * 2,
        [pltpu.VMEM(columns.shape, bf16),
         pltpu.VMEM(rows16.shape, f32), pltpu.VMEM(picked.shape, bf16),
         pltpu.VMEM((1, width), bf16), dma((4,))],
        parts, columns, rows16, picked, norm_gain, x_in, upstream,
    )
    for axis in ("xl", "core"):
        usage = usage + shifted(usage, axis, 1)
    counts, prob_sums = usage
    tokens_all = tokens * lax.axis_size(EXPERT_AXES)
    balance = EXPERTS * (counts / (tokens_all * TOPK)) * (prob_sums / tokens_all)
    return (fwd_out[None], bwd_out[None], balance[None])


def solution(mesh):
    sections = mesh.shape["section"]
    grid = mesh.devices.reshape(sections, -1, 2, 2)
    inner = Mesh(grid, ("section",) + EXPERT_AXES)
    rows = P("section", EXPERT_AXES, None)
    return jax.shard_map(
        body,
        mesh=inner,
        in_specs=(
            rows, rows, rows, rows, rows, rows, rows,
            P("section", None),
            P("section", None, EXPERT_AXES),
            P("section", None, EXPERT_AXES),
            rows,
        ),
        out_specs=(rows, rows, P("section", None)),
        check_vma=False,
    )
```

```python
import jax
import jax.numpy as jnp
from jax import lax
from jax.experimental import pallas as pl
from jax.experimental.pallas import tpu as pltpu
from jax.sharding import Mesh, PartitionSpec as P

EXPERTS = 128
TOPK = 8
EXP_WIN = 2
CAP = 8
SLOTS = EXP_WIN * CAP
EPS = 1e-06
exact = lax.Precision.HIGHEST
f32 = jnp.float32
bf16 = jnp.bfloat16
NT = (((1,), (1,)), ((), ()))
PARAMS = pltpu.CompilerParams(vmem_limit_bytes=48 << 20)
EXPERT_AXES = ("y", "xl", "core")
PAIR_DEVICES = 4


def shape(dims, dtype):
    return jax.ShapeDtypeStruct(dims, dtype)


def iota(dims, axis):
    return lax.broadcasted_iota(jnp.int32, dims, axis)


def hot_columns(routes_t, experts):
    ids = iota((experts, routes_t.shape[1]), 0)
    hot_t = jnp.zeros(ids.shape, f32)
    for k in range(TOPK):
        hot_t = hot_t + jnp.where(ids == routes_t[k : k + 1, :], 1.0, 0.0)
    return hot_t


def selection(hot_t):
    tokens = hot_t.shape[1]
    first = hot_t[0:8, :]
    before = jnp.where(iota((tokens, tokens), 0) < iota((tokens, tokens), 1), 1.0, 0.0)
    earlier = jnp.dot(first.astype(bf16), before.astype(bf16), preferred_element_type=f32)
    slot = iota((CAP, tokens), 0).astype(f32)
    return jnp.concatenate(
        [
            jnp.where((earlier[e : e + 1, :] == slot) & (first[e : e + 1, :] > 0.5), 1.0, 0.0)
            for e in range(EXP_WIN)
        ],
        axis=0,
    ).astype(bf16)


def slot_tables(routes_t, logits):
    tokens, experts = logits.shape
    hot_t = hot_columns(routes_t, experts)
    eye = jnp.where(iota((tokens, tokens), 0) == iota((tokens, tokens), 1), 1.0, 0.0).astype(bf16)
    hot = lax.dot_general(eye, hot_t.astype(bf16), NT, preferred_element_type=f32)
    chosen = jnp.where(hot > 0.5, logits, -jnp.inf)
    powers = jnp.exp(chosen - jnp.max(chosen, axis=1, keepdims=True))
    gates = powers / jnp.sum(powers, axis=1, keepdims=True)
    select = selection(hot_t)
    select_t = lax.dot_general(eye, select, NT, preferred_element_type=f32)
    picked = jnp.dot(select.astype(f32), gates, precision=exact, preferred_element_type=f32)
    own = iota((SLOTS, experts), 1) == iota((SLOTS, experts), 0) // CAP
    gate_slot = jnp.sum(jnp.where(own, picked, 0.0), axis=1, keepdims=True)
    return hot, select, select_t.astype(bf16), gate_slot


HBM = pl.BlockSpec(memory_space=pltpu.HBM)
VMEM = pl.BlockSpec(memory_space=pltpu.VMEM)


def in_hbm(dims, dtype):
    return pltpu.HBM(dims, dtype)


def kernel_call(body, outs, in_specs, out_specs, scratch, *args, us=2):
    args = [
        pltpu.with_memory_space_constraint(v, pltpu.HBM) if spec is HBM else v
        for v, spec in zip(args, in_specs)
    ]
    return pl.pallas_call(
        body, out_shape=outs, in_specs=in_specs, out_specs=out_specs, scratch_shapes=scratch,
        cost_estimate=pl.CostEstimate(flops=int(us * 1e9), transcendentals=0, bytes_accessed=0),
        compiler_params=PARAMS,
    )(*args)


def started(sems, *pairs):
    copies = [pltpu.make_async_copy(src, dst, sems.at[i]) for i, (src, dst) in enumerate(pairs)]
    for copy in copies:
        copy.start()
    return copies


def wait_all(copies):
    for copy in copies:
        copy.wait()


def in_parts(value):
    high = value.astype(bf16)
    rest = value - high.astype(f32)
    mid = rest.astype(bf16)
    return (rest - mid.astype(f32)).astype(bf16), mid, high


def normed_rows(rows, gain):
    inverse = lax.rsqrt(jnp.mean(rows * rows, axis=1, keepdims=True) + EPS)
    return (rows * inverse * gain).astype(bf16), inverse


def by_expert(stops):
    return [(i, i * EXP_WIN // stops * CAP) for i in range(stops)]


def usage_rows(counts, prob_sums):
    rows = [counts] + [p.astype(f32) for p in in_parts(prob_sums)]
    rows.append(jnp.zeros((CAP - len(rows), EXPERTS), f32))
    return jnp.concatenate(rows, axis=0).astype(bf16)


def usage_of(rows):
    rows = rows.astype(f32)
    return jnp.concatenate([rows[0:1, :], rows[1:2, :] + rows[2:3, :] + rows[3:4, :]], axis=0)


def prepare_body(
    saved_h, gain_h, broutes_h, blogits_h, froutes_h, flogits_h, gate_h, up_h, down_h,
    send, picked, columns, rows16, slab_h,
    saved, gain, broutes, blogits, froutes, flogits, usage, sems,
):
    hid = gate_h.shape[0]
    copies = started(
        sems, (broutes_h, broutes), (blogits_h, blogits), (froutes_h, froutes),
        (flogits_h, flogits), (gain_h, gain), (saved_h, saved),
        *[(w, slab_h.at[m * hid : (m + 1) * hid, :]) for m, w in enumerate((gate_h, up_h, down_h))],
    )
    wait_all(copies[:4])
    _, select, bselect_t, bgate = slot_tables(broutes[...], blogits[...])
    logits = flogits[...]
    hot, _, fselect_t, fgate = slot_tables(froutes[...], logits)
    powers = jnp.exp(logits - jnp.max(logits, axis=1, keepdims=True))
    probs = powers / jnp.sum(powers, axis=1, keepdims=True)
    usage[...] = usage_rows(
        jnp.sum(hot, axis=0, keepdims=True), jnp.sum(probs, axis=0, keepdims=True)
    )
    last = pltpu.make_async_copy(
        usage, slab_h.at[3 * hid : 3 * hid + CAP, 0:EXPERTS], sems.at[len(copies)]
    )
    last.start()
    wait_all(copies[4:6])
    rows = jnp.dot(select, saved[...], preferred_element_type=f32)
    normed, inverse = normed_rows(rows, gain[...].astype(f32))
    picked[...] = rows.astype(bf16)
    columns[0, :, :] = bselect_t
    columns[1, :, :] = fselect_t
    wide = (SLOTS, EXPERTS)
    rows16[0, :, :] = jnp.broadcast_to(bgate, wide)
    rows16[1, :, :] = jnp.broadcast_to(fgate, wide)
    rows16[2, :, :] = jnp.broadcast_to(inverse, wide)
    for i, r in by_expert(send.shape[0]):
        send[i, :, :] = normed[r : r + CAP, :]
    wait_all(copies[6:] + [last])


def rows_body(x_in, upstream, columns_h, rows16_h, gain_h, send, columns, gates, gain, sems):
    copies = started(sems, (columns_h, columns), (rows16_h.at[0], gates), (gain_h, gain))
    copies[0].wait()

    def chosen(i, block):
        return lax.dot_general(
            columns[i, :, :], block[...], (((0,), (0,)), ((), ())), preferred_element_type=f32
        )

    rows = chosen(1, x_in)
    grads = chosen(0, upstream)
    wait_all(copies[1:])
    normed = normed_rows(rows, gain[...].astype(f32))[0]
    grads = (grads * gates[:, 0:1]).astype(bf16)
    for i, r in by_expert(send.shape[0]):
        send[i, 0:CAP, :] = normed[r : r + CAP, :]
        send[i, CAP : 2 * CAP, :] = grads[r : r + CAP, :]


COLS = 512


def nt(a, b):
    return lax.dot_general(a, b, NT, preferred_element_type=f32)


def row_blocks(mixed_h, start, dst):
    return [
        (mixed_h.at[i, start : start + CAP, :], dst.at[i * CAP : (i + 1) * CAP, :])
        for i in range(mixed_h.shape[0])
    ]


def stacked(dst, *blocks):
    pairs, row = [], 0
    for block in blocks:
        pairs.append((block, dst.at[row : row + block.shape[0], :]))
        row += block.shape[0]
    return pairs


def hidden_of(pre):
    half, hid = pre.shape[0] // 2, pre.shape[1] // 2
    a, b = pre[:half, :hid], pre[:half, hid:]
    return (jax.nn.silu(a) * b).astype(bf16), pre[half:, :hid], pre[half:, hid:]


def hidden_grads(a, b, d_hidden):
    sigma = jax.nn.sigmoid(a)
    d_gate = d_hidden * b * sigma * (1.0 + a * (1.0 - sigma))
    d_up = d_hidden * a * sigma
    return jnp.concatenate([d_gate, d_up], axis=1).astype(bf16)


def slab_pairs(slabs, gu, down):
    hid = down.shape[0] // len(slabs)
    return (
        stacked(gu, *[w.at[0 : 2 * hid, :] for w in slabs]),
        stacked(down, *[w.at[2 * hid : 3 * hid, :] for w in slabs]),
    )


def tail_of(slab):
    return slab.at[slab.shape[0] - CAP :, 0:EXPERTS]


def row_pairs(mixed_h, saved_h, both, grads):
    first = row_blocks(mixed_h, 0, both) + [(saved_h, both.at[both.shape[0] // 2 :, :])]
    return first, row_blocks(mixed_h, CAP, grads)


def terms_of(both, grads, gate_up, down):
    h, a, b = hidden_of(nt(both[...], gate_up))
    return h, hidden_grads(a, b, nt(grads[...], down))


def expert_own_body(
    mixed_h, saved_h, slab0, slab1, first, usage, both, grads, tails, gu, down, sems
):
    width, hid = both.shape[1], down.shape[0] // 2
    early, late = row_pairs(mixed_h, saved_h, both, grads)
    gates, downs = slab_pairs((slab0, slab1), gu, down)
    early, late = early + gates, late + downs
    late += [(tail_of(w), tails.at[m]) for m, w in enumerate((slab0, slab1))]
    copies = started(sems, *early, *late)
    wait_all(copies)
    sides = [
        terms_of(both, grads, gu[2 * hid * m : 2 * hid * (m + 1), :], down[hid * m : hid * (m + 1), :])
        for m in range(2)
    ]
    h, terms = (jnp.concatenate(v, axis=1) for v in zip(*sides))
    for c in range(0, width, COLS):
        cut = slice(c, c + COLS)
        first[0, :, cut] = jnp.dot(h, down[:, cut], preferred_element_type=f32)
        first[1, :, cut] = jnp.dot(terms, gu[:, cut], preferred_element_type=f32)
    usage[...] = usage_of(tails[0]) + usage_of(tails[1])


def expert_terms_body(mixed_h, saved_h, slab, h, terms, both, grads, gu, down, sems):
    early, late = row_pairs(mixed_h, saved_h, both, grads)
    gates, downs = slab_pairs((slab,), gu, down)
    wait_all(started(sems, *early, *gates, *late, *downs))
    h[...], terms[...] = terms_of(both, grads, gu[...], down[...])


def expert_beside_body(
    mixed_h, saved_h, slab0, slab1, h0, terms0, usage, first_h, out,
    both, grads, tails, first, gu, down, sems,
):
    width, hid = both.shape[1], down.shape[0] // 2
    early, late = row_pairs(mixed_h, saved_h, both, grads)
    gates, downs = slab_pairs((slab0, slab1), gu, down)
    early += gates[1:] + late + downs[1:]
    late = gates[:1] + downs[:1] + [(first_h, first)]
    late += [(tail_of(w), tails.at[m]) for m, w in enumerate((slab0, slab1))]
    copies = started(sems, *early, *late)
    wait_all(copies[: len(early)])
    h1, terms1 = terms_of(both, grads, gu[2 * hid :, :], down[hid:, :])
    h = jnp.concatenate([h0[...], h1], axis=1)
    terms = jnp.concatenate([terms0[...], terms1], axis=1)
    wait_all(copies[len(early) :])
    for c in range(0, width, COLS):
        cut = slice(c, c + COLS)
        fwd = first[0, :, cut] + jnp.dot(h, down[:, cut], preferred_element_type=f32)
        bwd = first[1, :, cut] + jnp.dot(terms, gu[:, cut], preferred_element_type=f32)
        for i in range(out.shape[0]):
            out[i, 0:CAP, cut] = fwd[i * CAP : (i + 1) * CAP, :].astype(bf16)
            out[i, CAP : 2 * CAP, cut] = bwd[i * CAP : (i + 1) * CAP, :].astype(bf16)
    total = usage[...] + (usage_of(tails[0]) + usage_of(tails[1]))
    rows = usage_rows(total[0:1, :], total[1:2, :])
    for i in range(out.shape[0]):
        out[i, 0:CAP, width:] = rows
        out[i, CAP : 2 * CAP, width:] = jnp.zeros_like(rows)


def placed(select_t, rows):
    return sum(jnp.dot(select_t, p, preferred_element_type=f32) for p in in_parts(rows))


def combine_body(
    parts, columns_h, rows16_h, picked_h, gain_h, x_in, upstream, fwd_out, bwd_out, balance,
    columns, rows16, picked, gain, sems,
):
    wait_all(
        started(
            sems, (columns_h, columns), (rows16_h, rows16), (picked_h, picked), (gain_h, gain)
        )
    )
    half, width = parts.shape[0] // EXP_WIN, x_in.shape[1]

    def summed(start):
        return jnp.concatenate(
            [
                sum(
                    parts[e * half + i, start : start + CAP, 0:width].astype(f32)
                    for i in range(half)
                )
                for e in range(EXP_WIN)
            ],
            axis=0,
        )

    rows = summed(0) * rows16[1, :, 0:1]
    fwd_out[...] = (x_in[...].astype(f32) + placed(columns[1, :, :], rows)).astype(bf16)
    weighted = gain[...].astype(f32) * summed(CAP)
    inv = rows16[2, :, 0:1]
    x = picked[...].astype(f32)
    rows = inv * weighted - x * (inv * inv * inv) * jnp.mean(x * weighted, axis=1, keepdims=True)
    bwd_out[...] = (upstream[...].astype(f32) + placed(columns[0, :, :], rows)).astype(bf16)
    usage = usage_of(parts[0, 0:CAP, width:])
    for i in range(1, parts.shape[0]):
        usage = usage + usage_of(parts[i, 0:CAP, width:])
    tokens_all = x_in.shape[0] * parts.shape[0] * PAIR_DEVICES
    balance[...] = EXPERTS * (usage[0:1, :] / (tokens_all * TOPK)) * (usage[1:2, :] / tokens_all)


def shifted(block, axis, distance):
    n = lax.axis_size(axis)
    return lax.ppermute(block, axis, [((i - distance) % n, i) for i in range(n)])


def over_y(block):
    return lax.all_to_all(block, "y", split_axis=0, concat_axis=0, tiled=True)


def body(
    fwd_sent, bwd_sent, bwd_saved, fwd_routes, bwd_routes, fwd_logits, bwd_logits,
    norm_gain, w_gate, w_up, w_down,
):
    stops = lax.axis_size("y")
    tokens, width = fwd_sent.shape[1:]
    dma = pltpu.SemaphoreType.DMA
    upstream = shifted(bwd_sent[0], "section", -1)
    x_in = shifted(fwd_sent[0], "section", 1)
    hid = w_down.shape[1]
    saved_send, picked, columns, rows16, slab = kernel_call(
        prepare_body,
        (in_hbm((stops, CAP, width), bf16), in_hbm((SLOTS, width), bf16),
         in_hbm((EXP_WIN, tokens, SLOTS), bf16), in_hbm((3, SLOTS, EXPERTS), f32),
         in_hbm((3 * hid + CAP, width), bf16)),
        [HBM] * 9, [VMEM] * 4 + [HBM],
        [pltpu.VMEM((tokens, width), bf16), pltpu.VMEM((1, width), bf16),
         pltpu.VMEM((TOPK, tokens), jnp.int32), pltpu.VMEM((tokens, EXPERTS), f32),
         pltpu.VMEM((TOPK, tokens), jnp.int32), pltpu.VMEM((tokens, EXPERTS), f32),
         pltpu.VMEM((CAP, EXPERTS), bf16), dma((10,))],
        bwd_saved[0], norm_gain, bwd_routes[0].T, bwd_logits[0], fwd_routes[0].T, fwd_logits[0],
        w_gate[0].T, w_up[0].T, w_down[0],
    )
    slab_x = shifted(slab, "xl", 1)
    slab_core = shifted(slab, "core", 1)
    saved_all = over_y(saved_send).reshape(-1, width)
    mixed_send = kernel_call(
        rows_body, in_hbm((stops, 2 * CAP, width), bf16), [VMEM, VMEM, HBM, HBM, HBM], VMEM,
        [pltpu.VMEM((EXP_WIN, tokens, SLOTS), bf16), pltpu.VMEM((SLOTS, EXPERTS), f32),
         pltpu.VMEM((1, width), bf16), dma((3,))],
        x_in, upstream, columns, rows16, norm_gain, us=5,
    )
    mixed_all = over_y(mixed_send)
    count = stops * CAP
    vmem = pltpu.VMEM
    both, grads = vmem((2 * count, width), bf16), vmem((count, width), bf16)
    gu, down = vmem((4 * hid, width), bf16), vmem((2 * hid, width), bf16)
    tails = vmem((2, CAP, EXPERTS), bf16)
    sums = in_hbm((2, count, width), f32)
    first, usage = kernel_call(
        expert_own_body, (sums, in_hbm((2, EXPERTS), f32)), [HBM] * 4, [VMEM] * 2,
        [both, grads, tails, gu, down, dma((2 * stops + 8,))],
        mixed_all, saved_all, slab, slab_core, us=2,
    )
    slab_x, first = lax.optimization_barrier((slab_x, first))
    slab_x_core = shifted(slab_x, "core", 1)
    h, terms = kernel_call(
        expert_terms_body, (shape((count, hid), bf16), shape((count, 2 * hid), bf16)),
        [HBM] * 3, [VMEM] * 2,
        [both, grads, vmem((2 * hid, width), bf16), vmem((hid, width), bf16),
         dma((2 * stops + 8,))],
        mixed_all, saved_all, slab_x,
    )
    result = kernel_call(
        expert_beside_body, in_hbm((stops, 2 * CAP, width + EXPERTS), bf16),
        [HBM] * 3 + [VMEM] * 4 + [HBM], VMEM,
        [both, grads, tails, vmem(sums.shape, f32), gu, down, dma((2 * stops + 8,))],
        mixed_all, saved_all, slab_x, slab_x_core, h, terms, usage, first,
    )
    parts = over_y(result)
    full = in_hbm((tokens, width), bf16)
    fwd_out, bwd_out, balance = kernel_call(
        combine_body, (full, full, in_hbm((1, EXPERTS), f32)), [VMEM] + [HBM] * 4 + [VMEM] * 2, [VMEM] * 3,
        [pltpu.VMEM(columns.shape, bf16),
         pltpu.VMEM(rows16.shape, f32), pltpu.VMEM(picked.shape, bf16),
         pltpu.VMEM((1, width), bf16), dma((4,))],
        parts, columns, rows16, picked, norm_gain, x_in, upstream,
    )
    return (fwd_out[None], bwd_out[None], balance)


def solution(mesh):
    sections = mesh.shape["section"]
    grid = mesh.devices.reshape(sections, -1, 2, 2)
    inner = Mesh(grid, ("section",) + EXPERT_AXES)
    rows = P("section", EXPERT_AXES, None)
    return jax.shard_map(
        body,
        mesh=inner,
        in_specs=(
            rows, rows, rows, rows, rows, rows, rows,
            P("section", None),
            P("section", None, EXPERT_AXES),
            P("section", None, EXPERT_AXES),
            rows,
        ),
        out_specs=(rows, rows, P("section", None)),
        check_vma=False,
    )
```

```python
import jax
import jax.numpy as jnp
from jax import lax
from jax.experimental import pallas as pl
from jax.experimental.pallas import tpu as pltpu
from jax.sharding import Mesh, PartitionSpec as P

EXPERTS = 128
TOPK = 8
EXP_WIN = 2
CAP = 8
SLOTS = EXP_WIN * CAP
EPS = 1e-06
exact = lax.Precision.HIGHEST
f32 = jnp.float32
bf16 = jnp.bfloat16
NT = (((1,), (1,)), ((), ()))
PARAMS = pltpu.CompilerParams(vmem_limit_bytes=32 << 20)
EXPERT_AXES = ("y", "xl", "core")
PAIR_DEVICES = 4


def shape(dims, dtype):
    return jax.ShapeDtypeStruct(dims, dtype)


def iota(dims, axis):
    return lax.broadcasted_iota(jnp.int32, dims, axis)


def hot_columns(routes_t, experts):
    ids = iota((experts, routes_t.shape[1]), 0)
    hot_t = jnp.zeros(ids.shape, f32)
    for k in range(TOPK):
        hot_t = hot_t + jnp.where(ids == routes_t[k : k + 1, :], 1.0, 0.0)
    return hot_t


def selection(hot_t):
    tokens = hot_t.shape[1]
    first = hot_t[0:8, :]
    before = jnp.where(iota((tokens, tokens), 0) < iota((tokens, tokens), 1), 1.0, 0.0)
    earlier = jnp.dot(first.astype(bf16), before.astype(bf16), preferred_element_type=f32)
    slot = iota((CAP, tokens), 0).astype(f32)
    return jnp.concatenate(
        [
            jnp.where((earlier[e : e + 1, :] == slot) & (first[e : e + 1, :] > 0.5), 1.0, 0.0)
            for e in range(EXP_WIN)
        ],
        axis=0,
    ).astype(bf16)


def slot_tables(routes_t, logits):
    tokens, experts = logits.shape
    hot_t = hot_columns(routes_t, experts)
    eye = jnp.where(iota((tokens, tokens), 0) == iota((tokens, tokens), 1), 1.0, 0.0).astype(bf16)
    hot = lax.dot_general(eye, hot_t.astype(bf16), NT, preferred_element_type=f32)
    chosen = jnp.where(hot > 0.5, logits, -jnp.inf)
    powers = jnp.exp(chosen - jnp.max(chosen, axis=1, keepdims=True))
    gates = powers / jnp.sum(powers, axis=1, keepdims=True)
    select = selection(hot_t)
    select_t = lax.dot_general(eye, select, NT, preferred_element_type=f32)
    picked = jnp.dot(select.astype(f32), gates, precision=exact, preferred_element_type=f32)
    own = iota((SLOTS, experts), 1) == iota((SLOTS, experts), 0) // CAP
    gate_slot = jnp.sum(jnp.where(own, picked, 0.0), axis=1, keepdims=True)
    return hot, select, select_t.astype(bf16), gate_slot


HBM = pl.BlockSpec(memory_space=pltpu.HBM)
VMEM = pl.BlockSpec(memory_space=pltpu.VMEM)
PINNED = pl.BlockSpec(memory_space=pltpu.VMEM)


def in_hbm(dims, dtype):
    return pltpu.HBM(dims, dtype)


def in_vmem(dims, dtype):
    return pltpu.VMEM(dims, dtype)


def kernel_call(body, outs, in_specs, out_specs, scratch, *args, us=2):
    args = [
        v if spec is VMEM
        else pltpu.with_memory_space_constraint(v, pltpu.HBM if spec is HBM else pltpu.VMEM)
        for v, spec in zip(args, in_specs)
    ]
    return pl.pallas_call(
        body, out_shape=outs, in_specs=in_specs, out_specs=out_specs, scratch_shapes=scratch,
        cost_estimate=pl.CostEstimate(flops=int(us * 1e9), transcendentals=0, bytes_accessed=0),
        compiler_params=PARAMS,
    )(*args)


def started(sems, *pairs):
    copies = [pltpu.make_async_copy(src, dst, sems.at[i]) for i, (src, dst) in enumerate(pairs)]
    for copy in copies:
        copy.start()
    return copies


def wait_all(copies):
    for copy in copies:
        copy.wait()


def in_parts(value):
    high = value.astype(bf16)
    rest = value - high.astype(f32)
    mid = rest.astype(bf16)
    return (rest - mid.astype(f32)).astype(bf16), mid, high


def normed_rows(rows, gain):
    inverse = lax.rsqrt(jnp.mean(rows * rows, axis=1, keepdims=True) + EPS)
    return (rows * inverse * gain).astype(bf16), inverse


def by_expert(stops):
    return [(i, i * EXP_WIN // stops * CAP) for i in range(stops)]


def usage_rows(counts, prob_sums):
    rows = [counts] + [p.astype(f32) for p in in_parts(prob_sums)]
    rows.append(jnp.zeros((CAP - len(rows), EXPERTS), f32))
    return jnp.concatenate(rows, axis=0).astype(bf16)


def usage_of(rows):
    rows = rows.astype(f32)
    return jnp.concatenate([rows[0:1, :], rows[1:2, :] + rows[2:3, :] + rows[3:4, :]], axis=0)


def prepare_body(
    saved_h, gain_h, broutes_h, blogits_h, froutes_h, flogits_h, gate_h, up_h, down_h,
    send, picked, columns, rows16, slab,
    saved, gain, broutes, blogits, froutes, flogits, sems,
):
    hid = gate_h.shape[0]
    copies = started(
        sems, (broutes_h, broutes), (blogits_h, blogits), (froutes_h, froutes),
        (flogits_h, flogits), (gain_h, gain), (saved_h, saved),
        *[(w, slab.at[m * hid : (m + 1) * hid, :]) for m, w in enumerate((gate_h, up_h, down_h))],
    )
    wait_all(copies[:4])
    _, select, bselect_t, bgate = slot_tables(broutes[...], blogits[...])
    logits = flogits[...]
    hot, _, fselect_t, fgate = slot_tables(froutes[...], logits)
    powers = jnp.exp(logits - jnp.max(logits, axis=1, keepdims=True))
    probs = powers / jnp.sum(powers, axis=1, keepdims=True)
    slab[3 * hid :, 0:EXPERTS] = usage_rows(
        jnp.sum(hot, axis=0, keepdims=True), jnp.sum(probs, axis=0, keepdims=True)
    )
    wait_all(copies[4:6])
    rows = jnp.dot(select, saved[...], preferred_element_type=f32)
    normed, inverse = normed_rows(rows, gain[...].astype(f32))
    picked[...] = rows.astype(bf16)
    columns[0, :, :] = bselect_t
    columns[1, :, :] = fselect_t
    wide = (SLOTS, EXPERTS)
    rows16[0, :, :] = jnp.broadcast_to(bgate, wide)
    rows16[1, :, :] = jnp.broadcast_to(fgate, wide)
    rows16[2, :, :] = jnp.broadcast_to(inverse, wide)
    for i, r in by_expert(send.shape[0]):
        send[i, :, :] = normed[r : r + CAP, :]
    wait_all(copies[6:])


def rows_body(x_in, upstream, columns_h, rows16_h, gain_h, send, columns, gates, gain, sems):
    copies = started(sems, (columns_h, columns), (rows16_h.at[0], gates), (gain_h, gain))
    copies[0].wait()

    def chosen(i, block):
        return lax.dot_general(
            columns[i, :, :], block[...], (((0,), (0,)), ((), ())), preferred_element_type=f32
        )

    rows = chosen(1, x_in)
    grads = chosen(0, upstream)
    wait_all(copies[1:])
    normed = normed_rows(rows, gain[...].astype(f32))[0]
    grads = (grads * gates[:, 0:1]).astype(bf16)
    for i, r in by_expert(send.shape[0]):
        send[i, 0:CAP, :] = normed[r : r + CAP, :]
        send[i, CAP : 2 * CAP, :] = grads[r : r + CAP, :]


COLS = 512


def nt(a, b):
    return lax.dot_general(a, b, NT, preferred_element_type=f32)


def row_blocks(mixed_h, start, dst):
    return [
        (mixed_h.at[i, start : start + CAP, :], dst.at[i * CAP : (i + 1) * CAP, :])
        for i in range(mixed_h.shape[0])
    ]


def stacked(dst, *blocks):
    pairs, row = [], 0
    for block in blocks:
        pairs.append((block, dst.at[row : row + block.shape[0], :]))
        row += block.shape[0]
    return pairs


def hidden_of(pre):
    half, hid = pre.shape[0] // 2, pre.shape[1] // 2
    a, b = pre[:half, :hid], pre[:half, hid:]
    return (jax.nn.silu(a) * b).astype(bf16), pre[half:, :hid], pre[half:, hid:]


def hidden_grads(a, b, d_hidden):
    sigma = jax.nn.sigmoid(a)
    d_gate = d_hidden * b * sigma * (1.0 + a * (1.0 - sigma))
    d_up = d_hidden * a * sigma
    return jnp.concatenate([d_gate, d_up], axis=1).astype(bf16)


def slab_pairs(slabs, gu, down):
    hid = down.shape[0] // len(slabs)
    return (
        stacked(gu, *[w.at[0 : 2 * hid, :] for w in slabs]),
        stacked(down, *[w.at[2 * hid : 3 * hid, :] for w in slabs]),
    )


def tail_of(slab):
    return slab.at[slab.shape[0] - CAP :, 0:EXPERTS]


def row_pairs(mixed_h, saved_h, both, grads):
    first = row_blocks(mixed_h, 0, both) + [(saved_h, both.at[both.shape[0] // 2 :, :])]
    return first, row_blocks(mixed_h, CAP, grads)


def terms_of(both, grads, gate_up, down):
    h, a, b = hidden_of(nt(both[...], gate_up))
    return h, hidden_grads(a, b, nt(grads[...], down))


def expert_own_body(
    mixed_h, saved_h, slab0, slab1, first, usage, both, grads, tails, gu, down, sems
):
    width, hid = both.shape[1], down.shape[0] // 2
    early, late = row_pairs(mixed_h, saved_h, both, grads)
    gates, downs = slab_pairs((slab0, slab1), gu, down)
    early, late = early + gates, late + downs
    late += [(tail_of(w), tails.at[m]) for m, w in enumerate((slab0, slab1))]
    copies = started(sems, *early, *late)
    wait_all(copies)
    sides = [
        terms_of(both, grads, gu[2 * hid * m : 2 * hid * (m + 1), :], down[hid * m : hid * (m + 1), :])
        for m in range(2)
    ]
    h, terms = (jnp.concatenate(v, axis=1) for v in zip(*sides))
    for c in range(0, width, COLS):
        cut = slice(c, c + COLS)
        first[0, :, cut] = jnp.dot(h, down[:, cut], preferred_element_type=f32)
        first[1, :, cut] = jnp.dot(terms, gu[:, cut], preferred_element_type=f32)
    usage[...] = usage_of(tails[0]) + usage_of(tails[1])


def expert_terms_body(mixed_h, saved_h, slab, h, terms, both, grads, gu, down, sems):
    early, late = row_pairs(mixed_h, saved_h, both, grads)
    gates, downs = slab_pairs((slab,), gu, down)
    wait_all(started(sems, *early, *gates, *late, *downs))
    h[...], terms[...] = terms_of(both, grads, gu[...], down[...])


def expert_beside_body(
    mixed_h, saved_h, slab0, slab1, h0, terms0, usage, first_h, out,
    both, grads, tails, first, gu, down, sems,
):
    width, hid = both.shape[1], down.shape[0] // 2
    early, late = row_pairs(mixed_h, saved_h, both, grads)
    gates, downs = slab_pairs((slab0, slab1), gu, down)
    early += gates[1:] + late + downs[1:]
    late = gates[:1] + downs[:1] + [(first_h, first)]
    late += [(tail_of(w), tails.at[m]) for m, w in enumerate((slab0, slab1))]
    copies = started(sems, *early, *late)
    wait_all(copies[: len(early)])
    h1, terms1 = terms_of(both, grads, gu[2 * hid :, :], down[hid:, :])
    h = jnp.concatenate([h0[...], h1], axis=1)
    terms = jnp.concatenate([terms0[...], terms1], axis=1)
    wait_all(copies[len(early) :])
    for c in range(0, width, COLS):
        cut = slice(c, c + COLS)
        fwd = first[0, :, cut] + jnp.dot(h, down[:, cut], preferred_element_type=f32)
        bwd = first[1, :, cut] + jnp.dot(terms, gu[:, cut], preferred_element_type=f32)
        for i in range(out.shape[0]):
            out[i, 0:CAP, cut] = fwd[i * CAP : (i + 1) * CAP, :].astype(bf16)
            out[i, CAP : 2 * CAP, cut] = bwd[i * CAP : (i + 1) * CAP, :].astype(bf16)
    total = usage[...] + (usage_of(tails[0]) + usage_of(tails[1]))
    rows = usage_rows(total[0:1, :], total[1:2, :])
    for i in range(out.shape[0]):
        out[i, 0:CAP, width:] = rows
        out[i, CAP : 2 * CAP, width:] = jnp.zeros_like(rows)


def placed(select_t, rows):
    return sum(jnp.dot(select_t, p, preferred_element_type=f32) for p in in_parts(rows))


def combine_body(
    parts, columns_h, rows16_h, picked_h, gain_h, x_in, upstream, fwd_out, bwd_out, balance,
    columns, rows16, picked, gain, sems,
):
    wait_all(
        started(
            sems, (columns_h, columns), (rows16_h, rows16), (picked_h, picked), (gain_h, gain)
        )
    )
    half, width = parts.shape[0] // EXP_WIN, x_in.shape[1]

    def summed(start):
        return jnp.concatenate(
            [
                sum(
                    parts[e * half + i, start : start + CAP, 0:width].astype(f32)
                    for i in range(half)
                )
                for e in range(EXP_WIN)
            ],
            axis=0,
        )

    rows = summed(0) * rows16[1, :, 0:1]
    fwd_out[...] = (x_in[...].astype(f32) + placed(columns[1, :, :], rows)).astype(bf16)
    weighted = gain[...].astype(f32) * summed(CAP)
    inv = rows16[2, :, 0:1]
    x = picked[...].astype(f32)
    rows = inv * weighted - x * (inv * inv * inv) * jnp.mean(x * weighted, axis=1, keepdims=True)
    bwd_out[...] = (upstream[...].astype(f32) + placed(columns[0, :, :], rows)).astype(bf16)
    usage = usage_of(parts[0, 0:CAP, width:])
    for i in range(1, parts.shape[0]):
        usage = usage + usage_of(parts[i, 0:CAP, width:])
    tokens_all = x_in.shape[0] * parts.shape[0] * PAIR_DEVICES
    balance[...] = EXPERTS * (usage[0:1, :] / (tokens_all * TOPK)) * (usage[1:2, :] / tokens_all)


def shifted(block, axis, distance):
    n = lax.axis_size(axis)
    return lax.ppermute(block, axis, [((i - distance) % n, i) for i in range(n)])


def over_y(block):
    return lax.all_to_all(block, "y", split_axis=0, concat_axis=0, tiled=True)


def body(
    fwd_sent, bwd_sent, bwd_saved, fwd_routes, bwd_routes, fwd_logits, bwd_logits,
    norm_gain, w_gate, w_up, w_down,
):
    stops = lax.axis_size("y")
    tokens, width = fwd_sent.shape[1:]
    dma = pltpu.SemaphoreType.DMA
    upstream = shifted(bwd_sent[0], "section", -1)
    x_in = shifted(fwd_sent[0], "section", 1)
    hid = w_down.shape[1]
    saved_send, picked, columns, rows16, slab = kernel_call(
        prepare_body,
        (in_vmem((stops, CAP, width), bf16), in_hbm((SLOTS, width), bf16),
         in_hbm((EXP_WIN, tokens, SLOTS), bf16), in_hbm((3, SLOTS, EXPERTS), f32),
         in_hbm((3 * hid + CAP, width), bf16)),
        [HBM] * 9, [VMEM] * 5,
        [pltpu.VMEM((tokens, width), bf16), pltpu.VMEM((1, width), bf16),
         pltpu.VMEM((TOPK, tokens), jnp.int32), pltpu.VMEM((tokens, EXPERTS), f32),
         pltpu.VMEM((TOPK, tokens), jnp.int32), pltpu.VMEM((tokens, EXPERTS), f32), dma((9,))],
        bwd_saved[0], norm_gain, bwd_routes[0].T, bwd_logits[0], fwd_routes[0].T, fwd_logits[0],
        w_gate[0].T, w_up[0].T, w_down[0],
    )
    slab_x = shifted(slab, "xl", 1)
    slab_core = shifted(slab, "core", 1)
    saved_all = over_y(saved_send).reshape(-1, width)
    mixed_send = kernel_call(
        rows_body, in_vmem((stops, 2 * CAP, width), bf16), [VMEM, VMEM, HBM, HBM, HBM], VMEM,
        [pltpu.VMEM((EXP_WIN, tokens, SLOTS), bf16), pltpu.VMEM((SLOTS, EXPERTS), f32),
         pltpu.VMEM((1, width), bf16), dma((3,))],
        x_in, upstream, columns, rows16, norm_gain, us=5,
    )
    mixed_all = over_y(mixed_send)
    count = stops * CAP
    vmem = pltpu.VMEM
    both, grads = vmem((2 * count, width), bf16), vmem((count, width), bf16)
    gu, down = vmem((4 * hid, width), bf16), vmem((2 * hid, width), bf16)
    tails = vmem((2, CAP, EXPERTS), bf16)
    sums = in_hbm((2, count, width), f32)
    first, usage = kernel_call(
        expert_own_body, (sums, in_hbm((2, EXPERTS), f32)), [PINNED, PINNED, HBM, HBM], [VMEM] * 2,
        [both, grads, tails, gu, down, dma((2 * stops + 8,))],
        mixed_all, saved_all, slab, slab_core, us=2,
    )
    slab_x, first = lax.optimization_barrier((slab_x, first))
    slab_x_core = shifted(slab_x, "core", 1)
    h, terms = kernel_call(
        expert_terms_body, (shape((count, hid), bf16), shape((count, 2 * hid), bf16)),
        [PINNED, PINNED, HBM], [VMEM] * 2,
        [both, grads, vmem((2 * hid, width), bf16), vmem((hid, width), bf16),
         dma((2 * stops + 8,))],
        mixed_all, saved_all, slab_x,
    )
    result = kernel_call(
        expert_beside_body, in_vmem((stops, 2 * CAP, width + EXPERTS), bf16),
        [PINNED, PINNED, HBM] + [VMEM] * 4 + [HBM], VMEM,
        [both, grads, tails, vmem(sums.shape, f32), gu, down, dma((2 * stops + 8,))],
        mixed_all, saved_all, slab_x, slab_x_core, h, terms, usage, first,
    )
    parts = over_y(result)
    full = in_hbm((tokens, width), bf16)
    fwd_out, bwd_out, balance = kernel_call(
        combine_body, (full, full, in_hbm((1, EXPERTS), f32)), [VMEM] + [HBM] * 4 + [VMEM] * 2, [VMEM] * 3,
        [pltpu.VMEM(columns.shape, bf16),
         pltpu.VMEM(rows16.shape, f32), pltpu.VMEM(picked.shape, bf16),
         pltpu.VMEM((1, width), bf16), dma((4,))],
        parts, columns, rows16, picked, norm_gain, x_in, upstream,
    )
    return (fwd_out[None], bwd_out[None], balance)


def solution(mesh):
    sections = mesh.shape["section"]
    grid = mesh.devices.reshape(sections, -1, 2, 2)
    inner = Mesh(grid, ("section",) + EXPERT_AXES)
    rows = P("section", EXPERT_AXES, None)
    return jax.shard_map(
        body,
        mesh=inner,
        in_specs=(
            rows, rows, rows, rows, rows, rows, rows,
            P("section", None),
            P("section", None, EXPERT_AXES),
            P("section", None, EXPERT_AXES),
            rows,
        ),
        out_specs=(rows, rows, P("section", None)),
        check_vma=False,
    )
```

```python
import jax
import jax.numpy as jnp
from jax import lax
from jax.experimental import pallas as pl
from jax.experimental.pallas import tpu as pltpu
from jax.sharding import Mesh, PartitionSpec as P

EXPERTS = 128
TOPK = 8
EXP_WIN = 2
CAP = 8
SLOTS = EXP_WIN * CAP
EPS = 1e-06
exact = lax.Precision.HIGHEST
f32 = jnp.float32
bf16 = jnp.bfloat16
NT = (((1,), (1,)), ((), ()))
PARAMS = pltpu.CompilerParams(vmem_limit_bytes=32 << 20)
EXPERT_AXES = ("y", "xl", "core")
PAIR_DEVICES = 4


def shape(dims, dtype):
    return jax.ShapeDtypeStruct(dims, dtype)


def iota(dims, axis):
    return lax.broadcasted_iota(jnp.int32, dims, axis)


def hot_columns(routes_t, experts):
    ids = iota((experts, routes_t.shape[1]), 0)
    hot_t = jnp.zeros(ids.shape, f32)
    for k in range(TOPK):
        hot_t = hot_t + jnp.where(ids == routes_t[k : k + 1, :], 1.0, 0.0)
    return hot_t


def selection(hot_t):
    tokens = hot_t.shape[1]
    first = hot_t[0:8, :]
    before = jnp.where(iota((tokens, tokens), 0) < iota((tokens, tokens), 1), 1.0, 0.0)
    earlier = jnp.dot(first.astype(bf16), before.astype(bf16), preferred_element_type=f32)
    slot = iota((CAP, tokens), 0).astype(f32)
    return jnp.concatenate(
        [
            jnp.where((earlier[e : e + 1, :] == slot) & (first[e : e + 1, :] > 0.5), 1.0, 0.0)
            for e in range(EXP_WIN)
        ],
        axis=0,
    ).astype(bf16)


def slot_tables(routes_t, logits):
    tokens, experts = logits.shape
    hot_t = hot_columns(routes_t, experts)
    eye = jnp.where(iota((tokens, tokens), 0) == iota((tokens, tokens), 1), 1.0, 0.0).astype(bf16)
    hot = lax.dot_general(eye, hot_t.astype(bf16), NT, preferred_element_type=f32)
    chosen = jnp.where(hot > 0.5, logits, -jnp.inf)
    powers = jnp.exp(chosen - jnp.max(chosen, axis=1, keepdims=True))
    gates = powers / jnp.sum(powers, axis=1, keepdims=True)
    select = selection(hot_t)
    select_t = lax.dot_general(eye, select, NT, preferred_element_type=f32)
    picked = jnp.dot(select.astype(f32), gates, precision=exact, preferred_element_type=f32)
    own = iota((SLOTS, experts), 1) == iota((SLOTS, experts), 0) // CAP
    gate_slot = jnp.sum(jnp.where(own, picked, 0.0), axis=1, keepdims=True)
    return hot, select, select_t.astype(bf16), gate_slot


HBM = pl.BlockSpec(memory_space=pltpu.HBM)
VMEM = pl.BlockSpec(memory_space=pltpu.VMEM)
PINNED = pl.BlockSpec(memory_space=pltpu.VMEM)


def in_hbm(dims, dtype):
    return pltpu.HBM(dims, dtype)


def in_vmem(dims, dtype):
    return pltpu.VMEM(dims, dtype)


def kernel_call(body, outs, in_specs, out_specs, scratch, *args, us=2):
    args = [
        v if spec is VMEM
        else pltpu.with_memory_space_constraint(v, pltpu.HBM if spec is HBM else pltpu.VMEM)
        for v, spec in zip(args, in_specs)
    ]
    return pl.pallas_call(
        body, out_shape=outs, in_specs=in_specs, out_specs=out_specs, scratch_shapes=scratch,
        cost_estimate=pl.CostEstimate(flops=int(us * 1e9), transcendentals=0, bytes_accessed=0),
        compiler_params=PARAMS,
    )(*args)


def started(sems, *pairs):
    copies = [pltpu.make_async_copy(src, dst, sems.at[i]) for i, (src, dst) in enumerate(pairs)]
    for copy in copies:
        copy.start()
    return copies


def wait_all(copies):
    for copy in copies:
        copy.wait()


def in_parts(value):
    high = value.astype(bf16)
    rest = value - high.astype(f32)
    mid = rest.astype(bf16)
    return (rest - mid.astype(f32)).astype(bf16), mid, high


def normed_rows(rows, gain):
    inverse = lax.rsqrt(jnp.mean(rows * rows, axis=1, keepdims=True) + EPS)
    return (rows * inverse * gain).astype(bf16), inverse


def by_expert(stops):
    return [(i, i * EXP_WIN // stops * CAP) for i in range(stops)]


def usage_rows(counts, prob_sums):
    rows = [counts] + [p.astype(f32) for p in in_parts(prob_sums)]
    rows.append(jnp.zeros((CAP - len(rows), EXPERTS), f32))
    return jnp.concatenate(rows, axis=0).astype(bf16)


def usage_of(rows):
    rows = rows.astype(f32)
    return jnp.concatenate([rows[0:1, :], rows[1:2, :] + rows[2:3, :] + rows[3:4, :]], axis=0)


def prepare_body(
    saved_h, gain_h, broutes_h, blogits_h, froutes_h, flogits_h, gate_h, up_h, down_h,
    send, picked, columns, rows16, slab,
    saved, gain, broutes, blogits, froutes, flogits, sems,
):
    hid = gate_h.shape[0]
    copies = started(
        sems, (broutes_h, broutes), (blogits_h, blogits), (froutes_h, froutes),
        (flogits_h, flogits), (gain_h, gain), (saved_h, saved),
        *[(w, slab.at[m * hid : (m + 1) * hid, :]) for m, w in enumerate((gate_h, up_h, down_h))],
    )
    wait_all(copies[:4])
    _, select, bselect_t, bgate = slot_tables(broutes[...], blogits[...])
    logits = flogits[...]
    hot, _, fselect_t, fgate = slot_tables(froutes[...], logits)
    powers = jnp.exp(logits - jnp.max(logits, axis=1, keepdims=True))
    probs = powers / jnp.sum(powers, axis=1, keepdims=True)
    slab[3 * hid :, 0:EXPERTS] = usage_rows(
        jnp.sum(hot, axis=0, keepdims=True), jnp.sum(probs, axis=0, keepdims=True)
    )
    wait_all(copies[4:6])
    rows = jnp.dot(select, saved[...], preferred_element_type=f32)
    normed, inverse = normed_rows(rows, gain[...].astype(f32))
    picked[...] = rows.astype(bf16)
    columns[0, :, :] = bselect_t
    columns[1, :, :] = fselect_t
    wide = (SLOTS, EXPERTS)
    rows16[0, :, :] = jnp.broadcast_to(bgate, wide)
    rows16[1, :, :] = jnp.broadcast_to(fgate, wide)
    rows16[2, :, :] = jnp.broadcast_to(inverse, wide)
    for i, r in by_expert(send.shape[0]):
        send[i, :, :] = normed[r : r + CAP, :]
    wait_all(copies[6:])


def rows_body(
    x_in_h, upstream_h, columns_h, rows16_h, gain_h, send,
    columns, gates, gain, x_in, upstream, sems,
):
    copies = started(
        sems, (columns_h, columns), (rows16_h.at[0], gates), (gain_h, gain), (x_in_h, x_in),
        (upstream_h, upstream),
    )
    wait_all(copies)

    def chosen(i, block):
        return lax.dot_general(
            columns[i, :, :], block[...], (((0,), (0,)), ((), ())), preferred_element_type=f32
        )

    rows = chosen(1, x_in)
    grads = chosen(0, upstream)
    normed = normed_rows(rows, gain[...].astype(f32))[0]
    grads = (grads * gates[:, 0:1]).astype(bf16)
    for i, r in by_expert(send.shape[0]):
        send[i, 0:CAP, :] = normed[r : r + CAP, :]
        send[i, CAP : 2 * CAP, :] = grads[r : r + CAP, :]


COLS = 512


def nt(a, b):
    return lax.dot_general(a, b, NT, preferred_element_type=f32)


def row_blocks(mixed_h, start, dst):
    return [
        (mixed_h.at[i, start : start + CAP, :], dst.at[i * CAP : (i + 1) * CAP, :])
        for i in range(mixed_h.shape[0])
    ]


def stacked(dst, *blocks):
    pairs, row = [], 0
    for block in blocks:
        pairs.append((block, dst.at[row : row + block.shape[0], :]))
        row += block.shape[0]
    return pairs


def hidden_of(pre):
    half, hid = pre.shape[0] // 2, pre.shape[1] // 2
    a, b = pre[:half, :hid], pre[:half, hid:]
    return (jax.nn.silu(a) * b).astype(bf16), pre[half:, :hid], pre[half:, hid:]


def hidden_grads(a, b, d_hidden):
    sigma = jax.nn.sigmoid(a)
    d_gate = d_hidden * b * sigma * (1.0 + a * (1.0 - sigma))
    d_up = d_hidden * a * sigma
    return jnp.concatenate([d_gate, d_up], axis=1).astype(bf16)


def slab_pairs(slabs, gu, down):
    hid = down.shape[0] // len(slabs)
    return (
        stacked(gu, *[w.at[0 : 2 * hid, :] for w in slabs]),
        stacked(down, *[w.at[2 * hid : 3 * hid, :] for w in slabs]),
    )


def tail_of(slab):
    return slab.at[slab.shape[0] - CAP :, 0:EXPERTS]


def row_pairs(mixed_h, saved_h, both, grads):
    first = row_blocks(mixed_h, 0, both) + [(saved_h, both.at[both.shape[0] // 2 :, :])]
    return first, row_blocks(mixed_h, CAP, grads)


def terms_of(both, grads, gate_up, down):
    h, a, b = hidden_of(nt(both[...], gate_up))
    return h, hidden_grads(a, b, nt(grads[...], down))


def expert_own_body(
    mixed_h, saved_h, slab0, slab1, first, usage, both, grads, tails, gu, down, sems
):
    width, hid = both.shape[1], down.shape[0] // 2
    early, late = row_pairs(mixed_h, saved_h, both, grads)
    gates, downs = slab_pairs((slab0, slab1), gu, down)
    early, late = early + gates, late + downs
    late += [(tail_of(w), tails.at[m]) for m, w in enumerate((slab0, slab1))]
    copies = started(sems, *early, *late)
    wait_all(copies)
    sides = [
        terms_of(both, grads, gu[2 * hid * m : 2 * hid * (m + 1), :], down[hid * m : hid * (m + 1), :])
        for m in range(2)
    ]
    h, terms = (jnp.concatenate(v, axis=1) for v in zip(*sides))
    for c in range(0, width, COLS):
        cut = slice(c, c + COLS)
        first[0, :, cut] = jnp.dot(h, down[:, cut], preferred_element_type=f32)
        first[1, :, cut] = jnp.dot(terms, gu[:, cut], preferred_element_type=f32)
    usage[...] = usage_of(tails[0]) + usage_of(tails[1])


def added(both, grads, slab, sums):
    hid = (slab.shape[0] - CAP) // 3
    h, terms = terms_of(both, grads, slab[0 : 2 * hid, :], slab[2 * hid : 3 * hid, :])
    for c in range(0, both.shape[1], COLS):
        cut = slice(c, c + COLS)
        fwd = jnp.dot(h, slab[2 * hid : 3 * hid, cut], preferred_element_type=f32)
        bwd = jnp.dot(terms, slab[0 : 2 * hid, cut], preferred_element_type=f32)
        yield cut, sums[0, :, cut] + fwd, sums[1, :, cut] + bwd


def expert_beside_body(both, grads, slab, first, second):
    for cut, fwd, bwd in added(both, grads, slab, first):
        second[0, :, cut] = fwd
        second[1, :, cut] = bwd


def expert_last_body(both, grads, slab0, slab1, second, usage, out):
    width = both.shape[1]
    for cut, fwd, bwd in added(both, grads, slab1, second):
        for i in range(out.shape[0]):
            out[i, 0:CAP, cut] = fwd[i * CAP : (i + 1) * CAP, :].astype(bf16)
            out[i, CAP : 2 * CAP, cut] = bwd[i * CAP : (i + 1) * CAP, :].astype(bf16)
    beside = [usage_of(tail_of(w)[...]) for w in (slab0, slab1)]
    total = usage[...] + (beside[0] + beside[1])
    rows = usage_rows(total[0:1, :], total[1:2, :])
    for i in range(out.shape[0]):
        out[i, 0:CAP, width:] = rows
        out[i, CAP : 2 * CAP, width:] = jnp.zeros_like(rows)


def placed(select_t, rows):
    parts = in_parts(rows)
    return jnp.dot(
        jnp.concatenate([select_t] * len(parts), axis=1),
        jnp.concatenate(parts, axis=0),
        preferred_element_type=f32,
    )


def combine_body(
    parts, columns_h, rows16_h, picked_h, gain_h, x_in_h, upstream_h, fwd_out, bwd_out, balance,
    columns, rows16, picked, gain, x_in, upstream, sems,
):
    copies = started(
        sems, (columns_h, columns), (rows16_h, rows16), (picked_h, picked), (gain_h, gain),
        (x_in_h, x_in), (upstream_h, upstream),
    )
    wait_all(copies[:4])
    half, width = parts.shape[0] // EXP_WIN, x_in.shape[1]

    def summed(start):
        return jnp.concatenate(
            [
                sum(
                    parts[e * half + i, start : start + CAP, 0:width].astype(f32)
                    for i in range(half)
                )
                for e in range(EXP_WIN)
            ],
            axis=0,
        )

    rows = summed(0) * rows16[1, :, 0:1]
    wait_all(copies[4:])
    fwd_out[...] = (x_in[...].astype(f32) + placed(columns[1, :, :], rows)).astype(bf16)
    weighted = gain[...].astype(f32) * summed(CAP)
    inv = rows16[2, :, 0:1]
    x = picked[...].astype(f32)
    rows = inv * weighted - x * (inv * inv * inv) * jnp.mean(x * weighted, axis=1, keepdims=True)
    bwd_out[...] = (upstream[...].astype(f32) + placed(columns[0, :, :], rows)).astype(bf16)
    usage = usage_of(parts[0, 0:CAP, width:])
    for i in range(1, parts.shape[0]):
        usage = usage + usage_of(parts[i, 0:CAP, width:])
    tokens_all = x_in.shape[0] * parts.shape[0] * PAIR_DEVICES
    balance[...] = EXPERTS * (usage[0:1, :] / (tokens_all * TOPK)) * (usage[1:2, :] / tokens_all)


def shifted(block, axis, distance):
    n = lax.axis_size(axis)
    return lax.ppermute(block, axis, [((i - distance) % n, i) for i in range(n)])


def over_y(block):
    return lax.all_to_all(block, "y", split_axis=0, concat_axis=0, tiled=True)


def body(
    fwd_sent, bwd_sent, bwd_saved, fwd_routes, bwd_routes, fwd_logits, bwd_logits,
    norm_gain, w_gate, w_up, w_down,
):
    stops = lax.axis_size("y")
    tokens, width = fwd_sent.shape[1:]
    dma = pltpu.SemaphoreType.DMA
    upstream = shifted(bwd_sent[0], "section", -1)
    x_in = shifted(fwd_sent[0], "section", 1)
    hid = w_down.shape[1]
    saved_send, picked, columns, rows16, slab = kernel_call(
        prepare_body,
        (in_vmem((stops, CAP, width), bf16), in_hbm((SLOTS, width), bf16),
         in_hbm((EXP_WIN, tokens, SLOTS), bf16), in_hbm((3, SLOTS, EXPERTS), f32),
         in_hbm((3 * hid + CAP, width), bf16)),
        [HBM] * 9, [VMEM] * 5,
        [pltpu.VMEM((tokens, width), bf16), pltpu.VMEM((1, width), bf16),
         pltpu.VMEM((TOPK, tokens), jnp.int32), pltpu.VMEM((tokens, EXPERTS), f32),
         pltpu.VMEM((TOPK, tokens), jnp.int32), pltpu.VMEM((tokens, EXPERTS), f32), dma((9,))],
        bwd_saved[0], norm_gain, bwd_routes[0].T, bwd_logits[0], fwd_routes[0].T, fwd_logits[0],
        w_gate[0].T, w_up[0].T, w_down[0],
    )
    slab_x = shifted(slab, "xl", 1)
    slab_core = shifted(slab, "core", 1)
    saved_all = over_y(saved_send).reshape(-1, width)
    block = pltpu.VMEM((tokens, width), bf16)
    mixed_send = kernel_call(
        rows_body, in_vmem((stops, 2 * CAP, width), bf16), [HBM] * 5, VMEM,
        [pltpu.VMEM((EXP_WIN, tokens, SLOTS), bf16), pltpu.VMEM((SLOTS, EXPERTS), f32),
         pltpu.VMEM((1, width), bf16), block, block, dma((5,))],
        x_in, upstream, columns, rows16, norm_gain, us=5,
    )
    mixed_all = over_y(mixed_send)
    count = stops * CAP
    vmem = pltpu.VMEM
    sums = in_vmem((2, count, width), f32)
    first, usage, both, grads = kernel_call(
        expert_own_body,
        (sums, in_hbm((2, EXPERTS), f32), in_vmem((2 * count, width), bf16),
         in_vmem((count, width), bf16)),
        [PINNED, PINNED, HBM, HBM], [VMEM] * 4,
        [vmem((2, CAP, EXPERTS), bf16), vmem((4 * hid, width), bf16),
         vmem((2 * hid, width), bf16), dma((2 * stops + 8,))],
        mixed_all, saved_all, slab, slab_core, us=2,
    )
    slab_x, first = lax.optimization_barrier((slab_x, first))
    slab_x_core = shifted(slab_x, "core", 1)
    second = kernel_call(
        expert_beside_body, sums, [PINNED] * 4, VMEM, [], both, grads, slab_x, first
    )
    result = kernel_call(
        expert_last_body, in_vmem((stops, 2 * CAP, width + EXPERTS), bf16),
        [PINNED] * 5 + [VMEM], VMEM, [],
        both, grads, slab_x, slab_x_core, second, usage,
    )
    parts = over_y(result)
    full = in_hbm((tokens, width), bf16)
    fwd_out, bwd_out, balance = kernel_call(
        combine_body, (full, full, in_hbm((1, EXPERTS), f32)), [VMEM] + [HBM] * 6, [VMEM] * 3,
        [pltpu.VMEM(columns.shape, bf16),
         pltpu.VMEM(rows16.shape, f32), pltpu.VMEM(picked.shape, bf16),
         pltpu.VMEM((1, width), bf16), block, block, dma((6,))],
        parts, columns, rows16, picked, norm_gain, x_in, upstream,
    )
    return (fwd_out[None], bwd_out[None], balance)


def solution(mesh):
    sections = mesh.shape["section"]
    grid = mesh.devices.reshape(sections, -1, 2, 2)
    inner = Mesh(grid, ("section",) + EXPERT_AXES)
    rows = P("section", EXPERT_AXES, None)
    return jax.shard_map(
        body,
        mesh=inner,
        in_specs=(
            rows, rows, rows, rows, rows, rows, rows,
            P("section", None),
            P("section", None, EXPERT_AXES),
            P("section", None, EXPERT_AXES),
            rows,
        ),
        out_specs=(rows, rows, P("section", None)),
        check_vma=False,
    )
```

```python
import jax
import jax.numpy as jnp
from jax import lax
from jax.experimental import pallas as pl
from jax.experimental.pallas import tpu as pltpu
from jax.sharding import Mesh, PartitionSpec as P

EXPERTS = 128
TOPK = 8
EXP_WIN = 2
CAP = 8
SLOTS = EXP_WIN * CAP
EPS = 1e-06
exact = lax.Precision.HIGHEST
f32 = jnp.float32
bf16 = jnp.bfloat16
NT = (((1,), (1,)), ((), ()))
PARAMS = pltpu.CompilerParams(vmem_limit_bytes=32 << 20)
EXPERT_AXES = ("y", "xl", "core")
PAIR_DEVICES = 4


def shape(dims, dtype):
    return jax.ShapeDtypeStruct(dims, dtype)


def iota(dims, axis):
    return lax.broadcasted_iota(jnp.int32, dims, axis)


def hot_columns(routes_t, experts):
    ids = iota((experts, routes_t.shape[1]), 0)
    hot_t = jnp.zeros(ids.shape, f32)
    for k in range(TOPK):
        hot_t = hot_t + jnp.where(ids == routes_t[k : k + 1, :], 1.0, 0.0)
    return hot_t


def selection(hot_t):
    tokens = hot_t.shape[1]
    first = hot_t[0:8, :]
    before = jnp.where(iota((tokens, tokens), 0) < iota((tokens, tokens), 1), 1.0, 0.0)
    earlier = jnp.dot(first.astype(bf16), before.astype(bf16), preferred_element_type=f32)
    slot = iota((CAP, tokens), 0).astype(f32)
    return jnp.concatenate(
        [
            jnp.where((earlier[e : e + 1, :] == slot) & (first[e : e + 1, :] > 0.5), 1.0, 0.0)
            for e in range(EXP_WIN)
        ],
        axis=0,
    ).astype(bf16)


def slot_tables(routes_t, logits):
    tokens, experts = logits.shape
    hot_t = hot_columns(routes_t, experts)
    eye = jnp.where(iota((tokens, tokens), 0) == iota((tokens, tokens), 1), 1.0, 0.0).astype(bf16)
    hot = lax.dot_general(eye, hot_t.astype(bf16), NT, preferred_element_type=f32)
    chosen = jnp.where(hot > 0.5, logits, -jnp.inf)
    powers = jnp.exp(chosen - jnp.max(chosen, axis=1, keepdims=True))
    gates = powers / jnp.sum(powers, axis=1, keepdims=True)
    select = selection(hot_t)
    select_t = lax.dot_general(eye, select, NT, preferred_element_type=f32)
    picked = jnp.dot(select.astype(f32), gates, precision=exact, preferred_element_type=f32)
    own = iota((SLOTS, experts), 1) == iota((SLOTS, experts), 0) // CAP
    gate_slot = jnp.sum(jnp.where(own, picked, 0.0), axis=1, keepdims=True)
    return hot, select, select_t.astype(bf16), gate_slot


HBM = pl.BlockSpec(memory_space=pltpu.HBM)
VMEM = pl.BlockSpec(memory_space=pltpu.VMEM)
PINNED = pl.BlockSpec(memory_space=pltpu.VMEM)


def in_hbm(dims, dtype):
    return pltpu.HBM(dims, dtype)


def in_vmem(dims, dtype):
    return pltpu.VMEM(dims, dtype)


def kernel_call(body, outs, in_specs, out_specs, scratch, *args, us=2):
    args = [
        v if spec is VMEM
        else pltpu.with_memory_space_constraint(v, pltpu.HBM if spec is HBM else pltpu.VMEM)
        for v, spec in zip(args, in_specs)
    ]
    return pl.pallas_call(
        body, out_shape=outs, in_specs=in_specs, out_specs=out_specs, scratch_shapes=scratch,
        cost_estimate=pl.CostEstimate(flops=int(us * 1e9), transcendentals=0, bytes_accessed=0),
        compiler_params=PARAMS,
    )(*args)


def started(sems, *pairs):
    copies = [pltpu.make_async_copy(src, dst, sems.at[i]) for i, (src, dst) in enumerate(pairs)]
    for copy in copies:
        copy.start()
    return copies


def wait_all(copies):
    for copy in copies:
        copy.wait()


def in_parts(value):
    high = value.astype(bf16)
    rest = value - high.astype(f32)
    mid = rest.astype(bf16)
    return (rest - mid.astype(f32)).astype(bf16), mid, high


def normed_rows(rows, gain):
    inverse = lax.rsqrt(jnp.mean(rows * rows, axis=1, keepdims=True) + EPS)
    return (rows * inverse * gain).astype(bf16), inverse


def by_expert(stops):
    return [(i, i * EXP_WIN // stops * CAP) for i in range(stops)]


def usage_rows(counts, prob_sums):
    rows = [counts] + [p.astype(f32) for p in in_parts(prob_sums)]
    rows.append(jnp.zeros((CAP - len(rows), EXPERTS), f32))
    return jnp.concatenate(rows, axis=0).astype(bf16)


def usage_of(rows):
    rows = rows.astype(f32)
    return jnp.concatenate([rows[0:1, :], rows[1:2, :] + rows[2:3, :] + rows[3:4, :]], axis=0)


def prepare_body(
    saved_h, gain_h, broutes_h, blogits_h, froutes_h, flogits_h, gate_h, up_h, down_h,
    send, picked, columns, rows16, slab, usage,
    saved, gain, broutes, blogits, froutes, flogits, sems,
):
    hid = gate_h.shape[0]
    copies = started(
        sems, (broutes_h, broutes), (blogits_h, blogits), (froutes_h, froutes),
        (flogits_h, flogits), (gain_h, gain), (saved_h, saved),
        *[(w, slab.at[m * hid : (m + 1) * hid, :]) for m, w in enumerate((gate_h, up_h, down_h))],
    )
    wait_all(copies[:4])
    _, select, bselect_t, bgate = slot_tables(broutes[...], blogits[...])
    logits = flogits[...]
    hot, _, fselect_t, fgate = slot_tables(froutes[...], logits)
    powers = jnp.exp(logits - jnp.max(logits, axis=1, keepdims=True))
    probs = powers / jnp.sum(powers, axis=1, keepdims=True)
    usage[...] = jnp.concatenate(
        [jnp.sum(hot, axis=0, keepdims=True), jnp.sum(probs, axis=0, keepdims=True)], axis=0
    )
    wait_all(copies[4:6])
    rows = jnp.dot(select, saved[...], preferred_element_type=f32)
    normed, inverse = normed_rows(rows, gain[...].astype(f32))
    picked[...] = rows.astype(bf16)
    columns[0, :, :] = bselect_t
    columns[1, :, :] = fselect_t
    wide = (SLOTS, EXPERTS)
    rows16[0, :, :] = jnp.broadcast_to(bgate, wide)
    rows16[1, :, :] = jnp.broadcast_to(fgate, wide)
    rows16[2, :, :] = jnp.broadcast_to(inverse, wide)
    for i, r in by_expert(send.shape[0]):
        send[i, :, :] = normed[r : r + CAP, :]
    wait_all(copies[6:])


def rows_body(
    x_in_h, upstream_h, columns_h, rows16_h, gain_h, send,
    columns, gates, gain, x_in, upstream, sems,
):
    copies = started(
        sems, (columns_h, columns), (rows16_h.at[0], gates), (gain_h, gain), (x_in_h, x_in),
        (upstream_h, upstream),
    )
    wait_all(copies)

    def chosen(i, block):
        return lax.dot_general(
            columns[i, :, :], block[...], (((0,), (0,)), ((), ())), preferred_element_type=f32
        )

    rows = chosen(1, x_in)
    grads = chosen(0, upstream)
    normed = normed_rows(rows, gain[...].astype(f32))[0]
    grads = (grads * gates[:, 0:1]).astype(bf16)
    for i, r in by_expert(send.shape[0]):
        send[i, 0:CAP, :] = normed[r : r + CAP, :]
        send[i, CAP : 2 * CAP, :] = grads[r : r + CAP, :]


COLS = 512


def nt(a, b):
    return lax.dot_general(a, b, NT, preferred_element_type=f32)


def row_blocks(mixed_h, start, dst):
    return [
        (mixed_h.at[i, start : start + CAP, :], dst.at[i * CAP : (i + 1) * CAP, :])
        for i in range(mixed_h.shape[0])
    ]


def stacked(dst, *blocks):
    pairs, row = [], 0
    for block in blocks:
        pairs.append((block, dst.at[row : row + block.shape[0], :]))
        row += block.shape[0]
    return pairs


def hidden_of(pre):
    half, hid = pre.shape[0] // 2, pre.shape[1] // 2
    a, b = pre[:half, :hid], pre[:half, hid:]
    return (jax.nn.silu(a) * b).astype(bf16), pre[half:, :hid], pre[half:, hid:]


def hidden_grads(a, b, d_hidden):
    sigma = jax.nn.sigmoid(a)
    d_gate = d_hidden * b * sigma * (1.0 + a * (1.0 - sigma))
    d_up = d_hidden * a * sigma
    return jnp.concatenate([d_gate, d_up], axis=1).astype(bf16)


def row_pairs(mixed_h, saved_h, both, grads):
    first = row_blocks(mixed_h, 0, both) + [(saved_h, both.at[both.shape[0] // 2 :, :])]
    return first, row_blocks(mixed_h, CAP, grads)


def terms_of(both, grads, gate_up, down):
    h, a, b = hidden_of(nt(both[...], gate_up))
    return h, hidden_grads(a, b, nt(grads[...], down))


def expert_own_body(
    mixed_h, saved_h, slab0, slab1, usage0, usage1, first, usage, both, grads, sems
):
    early, late = row_pairs(mixed_h, saved_h, both, grads)
    wait_all(started(sems, *early, *late))
    for cut, fwd, bwd in added(both, grads, slab0, None):
        first[0, :, cut] = fwd
        first[1, :, cut] = bwd
    for cut, fwd, bwd in added(both, grads, slab1, first):
        first[0, :, cut] = fwd
        first[1, :, cut] = bwd
    usage[...] = usage0[...] + usage1[...]


def added(both, grads, slab, sums):
    hid = slab.shape[0] // 3
    h, terms = terms_of(both, grads, slab[0 : 2 * hid, :], slab[2 * hid : 3 * hid, :])
    for c in range(0, both.shape[1], COLS):
        cut = slice(c, c + COLS)
        fwd = jnp.dot(h, slab[2 * hid : 3 * hid, cut], preferred_element_type=f32)
        bwd = jnp.dot(terms, slab[0 : 2 * hid, cut], preferred_element_type=f32)
        if sums is None:
            yield cut, fwd, bwd
        else:
            yield cut, sums[0, :, cut] + fwd, sums[1, :, cut] + bwd


def expert_beside_body(both, grads, slab, first, second):
    for cut, fwd, bwd in added(both, grads, slab, first):
        second[0, :, cut] = fwd
        second[1, :, cut] = bwd


def expert_last_body(both, grads, slab, second, usage0, usage1, out):
    width = both.shape[1]
    for cut, fwd, bwd in added(both, grads, slab, second):
        for i in range(out.shape[0]):
            out[i, 0:CAP, cut] = fwd[i * CAP : (i + 1) * CAP, :].astype(bf16)
            out[i, CAP : 2 * CAP, cut] = bwd[i * CAP : (i + 1) * CAP, :].astype(bf16)
    total = usage0[...] + usage1[...]
    rows = usage_rows(total[0:1, :], total[1:2, :])
    for i in range(out.shape[0]):
        out[i, 0:CAP, width:] = rows
        out[i, CAP : 2 * CAP, width:] = jnp.zeros_like(rows)


def placed(select_t, rows):
    parts = in_parts(rows)
    return jnp.dot(
        jnp.concatenate([select_t] * len(parts), axis=1),
        jnp.concatenate(parts, axis=0),
        preferred_element_type=f32,
    )


def combine_body(
    parts, columns_h, rows16_h, picked_h, gain_h, x_in_h, upstream_h, fwd_out, bwd_out, balance,
    columns, rows16, picked, gain, x_in, upstream, sems,
):
    copies = started(
        sems, (columns_h, columns), (rows16_h, rows16), (picked_h, picked), (gain_h, gain),
        (x_in_h, x_in), (upstream_h, upstream),
    )
    wait_all(copies[:4])
    half, width = parts.shape[0] // EXP_WIN, x_in.shape[1]

    def summed(start):
        return jnp.concatenate(
            [
                sum(
                    parts[e * half + i, start : start + CAP, 0:width].astype(f32)
                    for i in range(half)
                )
                for e in range(EXP_WIN)
            ],
            axis=0,
        )

    rows = summed(0) * rows16[1, :, 0:1]
    wait_all(copies[4:])
    fwd_out[...] = (x_in[...].astype(f32) + placed(columns[1, :, :], rows)).astype(bf16)
    weighted = gain[...].astype(f32) * summed(CAP)
    inv = rows16[2, :, 0:1]
    x = picked[...].astype(f32)
    rows = inv * weighted - x * (inv * inv * inv) * jnp.mean(x * weighted, axis=1, keepdims=True)
    bwd_out[...] = (upstream[...].astype(f32) + placed(columns[0, :, :], rows)).astype(bf16)
    usage = usage_of(parts[0, 0:CAP, width:])
    for i in range(1, parts.shape[0]):
        usage = usage + usage_of(parts[i, 0:CAP, width:])
    tokens_all = x_in.shape[0] * parts.shape[0] * PAIR_DEVICES
    balance[...] = EXPERTS * (usage[0:1, :] / (tokens_all * TOPK)) * (usage[1:2, :] / tokens_all)


def shifted(block, axis, distance):
    n = lax.axis_size(axis)
    return lax.ppermute(block, axis, [((i - distance) % n, i) for i in range(n)])


def over_y(block):
    return lax.all_to_all(block, "y", split_axis=0, concat_axis=0, tiled=True)


def body(
    fwd_sent, bwd_sent, bwd_saved, fwd_routes, bwd_routes, fwd_logits, bwd_logits,
    norm_gain, w_gate, w_up, w_down,
):
    stops = lax.axis_size("y")
    tokens, width = fwd_sent.shape[1:]
    dma = pltpu.SemaphoreType.DMA
    upstream = shifted(bwd_sent[0], "section", -1)
    x_in = shifted(fwd_sent[0], "section", 1)
    hid = w_down.shape[1]
    saved_send, picked, columns, rows16, slab, usage = kernel_call(
        prepare_body,
        (in_vmem((stops, CAP, width), bf16), in_hbm((SLOTS, width), bf16),
         in_hbm((EXP_WIN, tokens, SLOTS), bf16), in_hbm((3, SLOTS, EXPERTS), f32),
         in_vmem((3 * hid, width), bf16), in_hbm((2, EXPERTS), f32)),
        [HBM] * 9, [VMEM] * 6,
        [pltpu.VMEM((tokens, width), bf16), pltpu.VMEM((1, width), bf16),
         pltpu.VMEM((TOPK, tokens), jnp.int32), pltpu.VMEM((tokens, EXPERTS), f32),
         pltpu.VMEM((TOPK, tokens), jnp.int32), pltpu.VMEM((tokens, EXPERTS), f32), dma((9,))],
        bwd_saved[0], norm_gain, bwd_routes[0].T, bwd_logits[0], fwd_routes[0].T, fwd_logits[0],
        w_gate[0].T, w_up[0].T, w_down[0],
    )
    slab_x = shifted(slab, "xl", 1)
    slab_core, usage_core = shifted(slab, "core", 1), shifted(usage, "core", 1)
    saved_all = over_y(saved_send).reshape(-1, width)
    block = pltpu.VMEM((tokens, width), bf16)
    rows16, usage_core = lax.optimization_barrier((rows16, usage_core))
    mixed_send = kernel_call(
        rows_body, in_vmem((stops, 2 * CAP, width), bf16), [HBM] * 5, VMEM,
        [pltpu.VMEM((EXP_WIN, tokens, SLOTS), bf16), pltpu.VMEM((SLOTS, EXPERTS), f32),
         pltpu.VMEM((1, width), bf16), block, block, dma((5,))],
        x_in, upstream, columns, rows16, norm_gain, us=5,
    )
    mixed_all = over_y(mixed_send)
    count = stops * CAP
    vmem = pltpu.VMEM
    sums = in_vmem((2, count, width), f32)
    first, usage_pair, both, grads = kernel_call(
        expert_own_body,
        (sums, in_hbm((2, EXPERTS), f32), in_vmem((2 * count, width), bf16),
         in_vmem((count, width), bf16)),
        [PINNED] * 4 + [VMEM] * 2, [VMEM] * 4, [dma((2 * stops + 1,))],
        mixed_all, saved_all, slab, slab_core, usage, usage_core, us=2,
    )
    slab_x, first = lax.optimization_barrier((slab_x, first))
    slab_x_core = shifted(slab_x, "core", 1)
    second = kernel_call(
        expert_beside_body, sums, [PINNED] * 4, VMEM, [], both, grads, slab_x, first
    )
    result = kernel_call(
        expert_last_body, in_vmem((stops, 2 * CAP, width + EXPERTS), bf16),
        [PINNED] * 4 + [VMEM] * 2, VMEM, [],
        both, grads, slab_x_core, second, usage_pair, shifted(usage_pair, "xl", 1),
    )
    parts = over_y(result)
    full = in_hbm((tokens, width), bf16)
    fwd_out, bwd_out, balance = kernel_call(
        combine_body, (full, full, in_hbm((1, EXPERTS), f32)), [VMEM] + [HBM] * 6, [VMEM] * 3,
        [pltpu.VMEM(columns.shape, bf16),
         pltpu.VMEM(rows16.shape, f32), pltpu.VMEM(picked.shape, bf16),
         pltpu.VMEM((1, width), bf16), block, block, dma((6,))],
        parts, columns, rows16, picked, norm_gain, x_in, upstream,
    )
    return (fwd_out[None], bwd_out[None], balance)


def solution(mesh):
    sections = mesh.shape["section"]
    grid = mesh.devices.reshape(sections, -1, 2, 2)
    inner = Mesh(grid, ("section",) + EXPERT_AXES)
    rows = P("section", EXPERT_AXES, None)
    return jax.shard_map(
        body,
        mesh=inner,
        in_specs=(
            rows, rows, rows, rows, rows, rows, rows,
            P("section", None),
            P("section", None, EXPERT_AXES),
            P("section", None, EXPERT_AXES),
            rows,
        ),
        out_specs=(rows, rows, P("section", None)),
        check_vma=False,
    )
```

```python
import jax
import jax.numpy as jnp
from jax import lax
from jax.experimental import pallas as pl
from jax.experimental.pallas import tpu as pltpu
from jax.sharding import Mesh, PartitionSpec as P

EXPERTS = 128
TOPK = 8
EXP_WIN = 2
CAP = 8
SLOTS = EXP_WIN * CAP
EPS = 1e-06
exact = lax.Precision.HIGHEST
f32 = jnp.float32
bf16 = jnp.bfloat16
NT = (((1,), (1,)), ((), ()))
PARAMS = pltpu.CompilerParams(vmem_limit_bytes=32 << 20)
EXPERT_AXES = ("y", "xl", "core")
PAIR_DEVICES = 4


def shape(dims, dtype):
    return jax.ShapeDtypeStruct(dims, dtype)


def iota(dims, axis):
    return lax.broadcasted_iota(jnp.int32, dims, axis)


def hot_columns(routes_t, experts):
    ids = iota((experts, routes_t.shape[1]), 0)
    hot_t = jnp.zeros(ids.shape, f32)
    for k in range(TOPK):
        hot_t = hot_t + jnp.where(ids == routes_t[k : k + 1, :], 1.0, 0.0)
    return hot_t


def selection(hot_t):
    tokens = hot_t.shape[1]
    first = hot_t[0:8, :]
    before = jnp.where(iota((tokens, tokens), 0) < iota((tokens, tokens), 1), 1.0, 0.0)
    earlier = jnp.dot(first.astype(bf16), before.astype(bf16), preferred_element_type=f32)
    slot = iota((CAP, tokens), 0).astype(f32)
    return jnp.concatenate(
        [
            jnp.where((earlier[e : e + 1, :] == slot) & (first[e : e + 1, :] > 0.5), 1.0, 0.0)
            for e in range(EXP_WIN)
        ],
        axis=0,
    ).astype(bf16)


def slot_tables(routes_t, logits):
    tokens, experts = logits.shape
    hot_t = hot_columns(routes_t, experts)
    eye = jnp.where(iota((tokens, tokens), 0) == iota((tokens, tokens), 1), 1.0, 0.0).astype(bf16)
    hot = lax.dot_general(eye, hot_t.astype(bf16), NT, preferred_element_type=f32)
    chosen = jnp.where(hot > 0.5, logits, -jnp.inf)
    powers = jnp.exp(chosen - jnp.max(chosen, axis=1, keepdims=True))
    gates = powers / jnp.sum(powers, axis=1, keepdims=True)
    select = selection(hot_t)
    select_t = lax.dot_general(eye, select, NT, preferred_element_type=f32)
    picked = jnp.dot(select.astype(f32), gates, precision=exact, preferred_element_type=f32)
    own = iota((SLOTS, experts), 1) == iota((SLOTS, experts), 0) // CAP
    gate_slot = jnp.sum(jnp.where(own, picked, 0.0), axis=1, keepdims=True)
    return hot, select, select_t.astype(bf16), gate_slot


HBM = pl.BlockSpec(memory_space=pltpu.HBM)
VMEM = pl.BlockSpec(memory_space=pltpu.VMEM)
PINNED = pl.BlockSpec(memory_space=pltpu.VMEM)


def in_hbm(dims, dtype):
    return pltpu.HBM(dims, dtype)


def in_vmem(dims, dtype):
    return pltpu.VMEM(dims, dtype)


def kernel_call(body, outs, in_specs, out_specs, scratch, *args, us=2):
    args = [
        v if spec is VMEM
        else pltpu.with_memory_space_constraint(v, pltpu.HBM if spec is HBM else pltpu.VMEM)
        for v, spec in zip(args, in_specs)
    ]
    return pl.pallas_call(
        body, out_shape=outs, in_specs=in_specs, out_specs=out_specs, scratch_shapes=scratch,
        cost_estimate=pl.CostEstimate(flops=int(us * 1e9), transcendentals=0, bytes_accessed=0),
        compiler_params=PARAMS,
    )(*args)


def started(sems, *pairs):
    copies = [pltpu.make_async_copy(src, dst, sems.at[i]) for i, (src, dst) in enumerate(pairs)]
    for copy in copies:
        copy.start()
    return copies


def wait_all(copies):
    for copy in copies:
        copy.wait()


def in_parts(value):
    high = value.astype(bf16)
    rest = value - high.astype(f32)
    mid = rest.astype(bf16)
    return (rest - mid.astype(f32)).astype(bf16), mid, high


def normed_rows(rows, gain):
    inverse = lax.rsqrt(jnp.mean(rows * rows, axis=1, keepdims=True) + EPS)
    return (rows * inverse * gain).astype(bf16), inverse


def by_expert(stops):
    return [(i, i * EXP_WIN // stops * CAP) for i in range(stops)]


def usage_rows(counts, prob_sums):
    rows = [counts] + [p.astype(f32) for p in in_parts(prob_sums)]
    rows.append(jnp.zeros((CAP - len(rows), EXPERTS), f32))
    return jnp.concatenate(rows, axis=0).astype(bf16)


def usage_of(rows):
    rows = rows.astype(f32)
    return jnp.concatenate([rows[0:1, :], rows[1:2, :] + rows[2:3, :] + rows[3:4, :]], axis=0)


def prepare_body(
    saved_h, gain_h, broutes_h, blogits_h, froutes_h, flogits_h, gate_h, up_h, down_h,
    send, picked, columns, rows16, slab, usage,
    saved, gain, broutes, blogits, froutes, flogits, sems,
):
    hid = gate_h.shape[0]
    copies = started(
        sems, (broutes_h, broutes), (blogits_h, blogits), (froutes_h, froutes),
        (flogits_h, flogits), (gain_h, gain), (saved_h, saved),
        *[(w, slab.at[m * hid : (m + 1) * hid, :]) for m, w in enumerate((gate_h, up_h, down_h))],
    )
    wait_all(copies[:4])
    _, select, bselect_t, bgate = slot_tables(broutes[...], blogits[...])
    logits = flogits[...]
    hot, _, fselect_t, fgate = slot_tables(froutes[...], logits)
    powers = jnp.exp(logits - jnp.max(logits, axis=1, keepdims=True))
    probs = powers / jnp.sum(powers, axis=1, keepdims=True)
    usage[...] = jnp.concatenate(
        [jnp.sum(hot, axis=0, keepdims=True), jnp.sum(probs, axis=0, keepdims=True)], axis=0
    )
    wait_all(copies[4:6])
    rows = jnp.dot(select, saved[...], preferred_element_type=f32)
    normed, inverse = normed_rows(rows, gain[...].astype(f32))
    picked[...] = rows.astype(bf16)
    columns[0, :, :] = bselect_t
    columns[1, :, :] = fselect_t
    wide = (SLOTS, EXPERTS)
    rows16[0, :, :] = jnp.broadcast_to(bgate, wide)
    rows16[1, :, :] = jnp.broadcast_to(fgate, wide)
    rows16[2, :, :] = jnp.broadcast_to(inverse, wide)
    for i, r in by_expert(send.shape[0]):
        send[i, :, :] = normed[r : r + CAP, :]
    wait_all(copies[6:])


def rows_body(
    x_in_h, upstream_h, columns_h, rows16_h, gain_h, send,
    columns, gates, gain, x_in, upstream, sems,
):
    copies = started(
        sems, (columns_h, columns), (rows16_h.at[0], gates), (gain_h, gain), (x_in_h, x_in),
        (upstream_h, upstream),
    )
    wait_all(copies)

    def chosen(i, block):
        return lax.dot_general(
            columns[i, :, :], block[...], (((0,), (0,)), ((), ())), preferred_element_type=f32
        )

    rows = chosen(1, x_in)
    grads = chosen(0, upstream)
    normed = normed_rows(rows, gain[...].astype(f32))[0]
    grads = (grads * gates[:, 0:1]).astype(bf16)
    for i, r in by_expert(send.shape[0]):
        send[i, 0:CAP, :] = normed[r : r + CAP, :]
        send[i, CAP : 2 * CAP, :] = grads[r : r + CAP, :]


COLS = 1024


def nt(a, b):
    return lax.dot_general(a, b, NT, preferred_element_type=f32)


def row_blocks(mixed_h, start, dst):
    return [
        (mixed_h.at[i, start : start + CAP, :], dst.at[i * CAP : (i + 1) * CAP, :])
        for i in range(mixed_h.shape[0])
    ]


def stacked(dst, *blocks):
    pairs, row = [], 0
    for block in blocks:
        pairs.append((block, dst.at[row : row + block.shape[0], :]))
        row += block.shape[0]
    return pairs


def hidden_of(pre):
    half, hid = pre.shape[0] // 2, pre.shape[1] // 2
    a, b = pre[:half, :hid], pre[:half, hid:]
    return (jax.nn.silu(a) * b).astype(bf16), pre[half:, :hid], pre[half:, hid:]


def hidden_grads(a, b, d_hidden):
    sigma = jax.nn.sigmoid(a)
    d_gate = d_hidden * b * sigma * (1.0 + a * (1.0 - sigma))
    d_up = d_hidden * a * sigma
    return jnp.concatenate([d_gate, d_up], axis=1).astype(bf16)


def row_pairs(mixed_h, saved_h, both, grads):
    first = row_blocks(mixed_h, 0, both) + [(saved_h, both.at[both.shape[0] // 2 :, :])]
    return first, row_blocks(mixed_h, CAP, grads)


def terms_of(both, grads, gate_up, down):
    h, a, b = hidden_of(nt(both[...], gate_up))
    return h, hidden_grads(a, b, nt(grads[...], down))


def expert_own_body(
    mixed_h, saved_h, slab0, slab1, usage0, usage1, first, usage, both, grads, sems
):
    early, late = row_pairs(mixed_h, saved_h, both, grads)
    wait_all(started(sems, *early, *late))
    for cut, fwd, bwd in added(both, grads, slab0, None):
        first[0, :, cut] = fwd
        first[1, :, cut] = bwd
    for cut, fwd, bwd in added(both, grads, slab1, first):
        first[0, :, cut] = fwd
        first[1, :, cut] = bwd
    usage[...] = usage0[...] + usage1[...]


def added(both, grads, slab, sums):
    hid = slab.shape[0] // 3
    h, terms = terms_of(both, grads, slab[0 : 2 * hid, :], slab[2 * hid : 3 * hid, :])
    for c in range(0, both.shape[1], COLS):
        cut = slice(c, c + COLS)
        fwd = jnp.dot(h, slab[2 * hid : 3 * hid, cut], preferred_element_type=f32)
        bwd = jnp.dot(terms, slab[0 : 2 * hid, cut], preferred_element_type=f32)
        if sums is None:
            yield cut, fwd, bwd
        else:
            yield cut, sums[0, :, cut] + fwd, sums[1, :, cut] + bwd


def expert_beside_body(both, grads, slab, first, second):
    for cut, fwd, bwd in added(both, grads, slab, first):
        second[0, :, cut] = fwd
        second[1, :, cut] = bwd


def expert_last_body(both, grads, slab, second, usage0, usage1, out):
    width = both.shape[1]
    for cut, fwd, bwd in added(both, grads, slab, second):
        for i in range(out.shape[0]):
            out[i, 0:CAP, cut] = fwd[i * CAP : (i + 1) * CAP, :].astype(bf16)
            out[i, CAP : 2 * CAP, cut] = bwd[i * CAP : (i + 1) * CAP, :].astype(bf16)
    total = usage0[...] + usage1[...]
    rows = usage_rows(total[0:1, :], total[1:2, :])
    for i in range(out.shape[0]):
        out[i, 0:CAP, width:] = rows
        out[i, CAP : 2 * CAP, width:] = jnp.zeros_like(rows)


def placed(select_t, rows):
    parts = in_parts(rows)
    return jnp.dot(
        jnp.concatenate([select_t] * len(parts), axis=1),
        jnp.concatenate(parts, axis=0),
        preferred_element_type=f32,
    )


def combine_body(
    parts, columns_h, rows16_h, picked_h, gain_h, x_in_h, upstream_h, fwd_out, bwd_out, balance,
    columns, rows16, picked, gain, x_in, upstream, sems,
):
    copies = started(
        sems, (columns_h, columns), (rows16_h, rows16), (picked_h, picked), (gain_h, gain),
        (x_in_h, x_in), (upstream_h, upstream),
    )
    wait_all(copies[:4])
    half, width = parts.shape[0] // EXP_WIN, x_in.shape[1]

    def summed(start):
        return jnp.concatenate(
            [
                sum(
                    parts[e * half + i, start : start + CAP, 0:width].astype(f32)
                    for i in range(half)
                )
                for e in range(EXP_WIN)
            ],
            axis=0,
        )

    rows = summed(0) * rows16[1, :, 0:1]
    wait_all(copies[4:])
    fwd_out[...] = (x_in[...].astype(f32) + placed(columns[1, :, :], rows)).astype(bf16)
    weighted = gain[...].astype(f32) * summed(CAP)
    inv = rows16[2, :, 0:1]
    x = picked[...].astype(f32)
    rows = inv * weighted - x * (inv * inv * inv) * jnp.mean(x * weighted, axis=1, keepdims=True)
    bwd_out[...] = (upstream[...].astype(f32) + placed(columns[0, :, :], rows)).astype(bf16)
    usage = usage_of(parts[0, 0:CAP, width:])
    for i in range(1, parts.shape[0]):
        usage = usage + usage_of(parts[i, 0:CAP, width:])
    tokens_all = x_in.shape[0] * parts.shape[0] * PAIR_DEVICES
    balance[...] = EXPERTS * (usage[0:1, :] / (tokens_all * TOPK)) * (usage[1:2, :] / tokens_all)


def shifted(block, axis, distance):
    n = lax.axis_size(axis)
    return lax.ppermute(block, axis, [((i - distance) % n, i) for i in range(n)])


def over_y(block):
    return lax.all_to_all(block, "y", split_axis=0, concat_axis=0, tiled=True)


def body(
    fwd_sent, bwd_sent, bwd_saved, fwd_routes, bwd_routes, fwd_logits, bwd_logits,
    norm_gain, w_gate, w_up, w_down,
):
    stops = lax.axis_size("y")
    tokens, width = fwd_sent.shape[1:]
    dma = pltpu.SemaphoreType.DMA
    upstream = shifted(bwd_sent[0], "section", -1)
    x_in = shifted(fwd_sent[0], "section", 1)
    hid = w_down.shape[1]
    saved_send, picked, columns, rows16, slab, usage = kernel_call(
        prepare_body,
        (in_vmem((stops, CAP, width), bf16), in_hbm((SLOTS, width), bf16),
         in_hbm((EXP_WIN, tokens, SLOTS), bf16), in_hbm((3, SLOTS, EXPERTS), f32),
         in_vmem((3 * hid, width), bf16), in_hbm((2, EXPERTS), f32)),
        [HBM] * 9, [VMEM] * 6,
        [pltpu.VMEM((tokens, width), bf16), pltpu.VMEM((1, width), bf16),
         pltpu.VMEM((TOPK, tokens), jnp.int32), pltpu.VMEM((tokens, EXPERTS), f32),
         pltpu.VMEM((TOPK, tokens), jnp.int32), pltpu.VMEM((tokens, EXPERTS), f32), dma((9,))],
        bwd_saved[0], norm_gain, bwd_routes[0].T, bwd_logits[0], fwd_routes[0].T, fwd_logits[0],
        w_gate[0].T, w_up[0].T, w_down[0],
    )
    slab_x = shifted(slab, "xl", 1)
    slab_core, usage_core = shifted(slab, "core", 1), shifted(usage, "core", 1)
    saved_all = over_y(saved_send).reshape(-1, width)
    block = pltpu.VMEM((tokens, width), bf16)
    rows16, usage_core = lax.optimization_barrier((rows16, usage_core))
    mixed_send = kernel_call(
        rows_body, in_vmem((stops, 2 * CAP, width), bf16), [HBM] * 5, VMEM,
        [pltpu.VMEM((EXP_WIN, tokens, SLOTS), bf16), pltpu.VMEM((SLOTS, EXPERTS), f32),
         pltpu.VMEM((1, width), bf16), block, block, dma((5,))],
        x_in, upstream, columns, rows16, norm_gain, us=5,
    )
    mixed_all = over_y(mixed_send)
    count = stops * CAP
    vmem = pltpu.VMEM
    sums = in_vmem((2, count, width), f32)
    first, usage_pair, both, grads = kernel_call(
        expert_own_body,
        (sums, in_hbm((2, EXPERTS), f32), in_vmem((2 * count, width), bf16),
         in_vmem((count, width), bf16)),
        [PINNED] * 4 + [VMEM] * 2, [VMEM] * 4, [dma((2 * stops + 1,))],
        mixed_all, saved_all, slab, slab_core, usage, usage_core, us=2,
    )
    slab_x, first = lax.optimization_barrier((slab_x, first))
    slab_x_core = shifted(slab_x, "core", 1)
    second = kernel_call(
        expert_beside_body, sums, [PINNED] * 4, VMEM, [], both, grads, slab_x, first
    )
    result = kernel_call(
        expert_last_body, in_vmem((stops, 2 * CAP, width + EXPERTS), bf16),
        [PINNED] * 4 + [VMEM] * 2, VMEM, [],
        both, grads, slab_x_core, second, usage_pair, shifted(usage_pair, "xl", 1),
    )
    parts = over_y(result)
    full = in_hbm((tokens, width), bf16)
    fwd_out, bwd_out, balance = kernel_call(
        combine_body, (full, full, in_hbm((1, EXPERTS), f32)), [VMEM] + [HBM] * 6, [VMEM] * 3,
        [pltpu.VMEM(columns.shape, bf16),
         pltpu.VMEM(rows16.shape, f32), pltpu.VMEM(picked.shape, bf16),
         pltpu.VMEM((1, width), bf16), block, block, dma((6,))],
        parts, columns, rows16, picked, norm_gain, x_in, upstream,
    )
    return (fwd_out[None], bwd_out[None], balance)


def solution(mesh):
    sections = mesh.shape["section"]
    grid = mesh.devices.reshape(sections, -1, 2, 2)
    inner = Mesh(grid, ("section",) + EXPERT_AXES)
    rows = P("section", EXPERT_AXES, None)
    return jax.shard_map(
        body,
        mesh=inner,
        in_specs=(
            rows, rows, rows, rows, rows, rows, rows,
            P("section", None),
            P("section", None, EXPERT_AXES),
            P("section", None, EXPERT_AXES),
            rows,
        ),
        out_specs=(rows, rows, P("section", None)),
        check_vma=False,
    )
```
